128 devices in a mesh: seq: 16 (over z, x), tp: 8 (over y, core).
Axes of the slice: x: 4, y: 4, z: 4, core: 2. Of those that a mesh axis runs over, the one named last changes fastest.
Arguments:
- queries: bfloat16 [16384, 8192], P('seq', 'tp'), may hold values from -0.29882812 to 0.29882812
- key_vectors: bfloat16 [16384, 8192], P('seq', 'tp'), may hold values from -0.29882812 to 0.29882812
- value_vectors: bfloat16 [16384, 8192], P('seq', 'tp'), may hold values from -0.29882812 to 0.29882812
- log_decay: float32 [64, 16384], P('tp', 'seq'), may hold values from -1 to 0
- grad_output: bfloat16 [16384, 6144], P('seq', 'tp'), may hold values from -6 to 6
- out_weight: bfloat16 [8192, 6144], P('tp'), may hold values from -0.0625 to 0.0625
Outputs:
- grad_queries: bfloat16 [16384, 8192], P('seq', 'tp')
- grad_keys: bfloat16 [16384, 8192], P('seq', 'tp')
- grad_values: bfloat16 [16384, 8192], P('seq', 'tp')
The draws below stay inside these ranges and needn't reach their ends.
All inputs are finite; a program needn't handle non-finite values.
Results may differ from the reference program's by a relative error of at most 0.0063.
Values may be sent and summed in bfloat16 or wider, within the bound.
A program may use at most 128 MiB of HBM per device.

```python
import math
import jax
import jax.numpy as jnp
from jax import lax

D = 6144
HEAD_COUNT = 64
HD = 128
BLK = 256
TOK_DEV = 1024
TOKEN_COUNT = 16384


def draw_log_decay(key, part):
    random_subkeys = jax.random.split(key, 6)
    chooser = jax.random.uniform(random_subkeys[0], (HEAD_COUNT,))
    slow_share = 0.5
    slow_mask = chooser < slow_share
    slow_rate = math.log(10.0) * jax.random.uniform(random_subkeys[1], (HEAD_COUNT,), minval=0.02, maxval=0.2) / TOKEN_COUNT
    fast_rate = 1.0 / jax.random.uniform(random_subkeys[2], (HEAD_COUNT,), minval=30.0, maxval=50.0)
    decay_rate = jnp.where(slow_mask, slow_rate, fast_rate)
    span_count = TOKEN_COUNT // TOK_DEV
    device_factor = jnp.exp(jax.random.uniform(random_subkeys[3], (HEAD_COUNT, span_count), minval=-math.log(2.0), maxval=math.log(2.0)))
    device_factor = jnp.repeat(device_factor, TOK_DEV, axis=1)
    baseline_decay = -decay_rate[:, None] * device_factor
    spike_positions = jax.random.randint(random_subkeys[4], (2,), 0, TOKEN_COUNT)
    spike_mask = jnp.any(jnp.arange(TOKEN_COUNT)[:, None] == spike_positions[None, :], axis=1)
    spike_decay_drop = jnp.log(jax.random.uniform(random_subkeys[5], (HEAD_COUNT, TOKEN_COUNT), minval=0.5, maxval=0.8))
    return jnp.where(spike_mask[None, :], baseline_decay + spike_decay_drop, baseline_decay).astype(jnp.float32)


def level_of(key, extent, cuts, least, largest):
    loudness, own = 1.0, jax.random.fold_in(key, 6)
    for dim, parts in cuts:
        steps = jnp.exp(jax.random.uniform(jax.random.fold_in(own, dim), (parts,), jnp.float32, least / len(cuts), largest / len(cuts)))
        loudness = loudness * jnp.repeat(steps, extent[dim] // parts).reshape([-1 if axis == dim else 1 for axis in range(len(extent))])
    return loudness


def centred(key, shape, spread, reach, cuts=(), held_as=jnp.bfloat16):
    result = spread * jax.random.normal(key, shape, jnp.float32)
    if cuts:
        result = result * level_of(key, shape, cuts, -0.22, 0.18)
    return jnp.clip(result, -reach, reach).astype(held_as)


def setup_inputs(seed: int = 0) -> dict:
    key_of = jax.random.split(jax.random.key(seed), 7)
    return {
        "queries": centred(key_of[0], (TOKEN_COUNT, HEAD_COUNT * HD), 0.05, 0.29882812, ((0, 16), (1, 8))),
        "key_vectors": centred(key_of[1], (TOKEN_COUNT, HEAD_COUNT * HD), 0.05, 0.29882812, ((0, 16), (1, 8))),
        "value_vectors": centred(key_of[2], (TOKEN_COUNT, HEAD_COUNT * HD), 0.05, 0.29882812, ((0, 16), (1, 8))),
        "log_decay": draw_log_decay(jax.random.fold_in(key_of[6], 71), 0),
        "grad_output": centred(key_of[4], (TOKEN_COUNT, D), 1.0, 6.0, ((0, 16), (1, 8))),
        "out_weight": centred(key_of[5], (HEAD_COUNT * HD, D), (HEAD_COUNT * HD) ** -0.5, 0.0625, ((0, 8),)),
    }


def contract(form, left, right):
    return jnp.einsum(form, left.astype(jnp.float32), right.astype(jnp.float32))


def key_sums(key_blk, value_blk, decay_blk):
    cum_decay = jnp.cumsum(decay_blk, axis=1)
    end_decay = cum_decay[:, -1]
    key_weight = jnp.exp(end_decay[:, None] - cum_decay).T
    key_scaled = (key_blk * key_weight[:, :, None]).astype(jnp.bfloat16)
    return contract("sha,shb->hab", key_scaled, value_blk), end_decay


def query_sums(query_blk, grad_blk, decay_blk):
    cum_decay = jnp.cumsum(decay_blk, axis=1)
    query_weight = jnp.exp(cum_decay).T
    query_scaled = (query_blk * query_weight[:, :, None]).astype(jnp.bfloat16)
    return contract("tha,thb->hab", query_scaled, grad_blk)


def block_terms(query_blk, key_blk, value_blk, grad_blk, decay_blk, enter_fwd, enter_bwd):
    blk_len = query_blk.shape[0]
    cum_decay = jnp.cumsum(decay_blk, axis=1)
    end_decay = cum_decay[:, -1]
    causal = (jnp.arange(blk_len)[:, None] >= jnp.arange(blk_len)[None, :])[None]
    gap_decay = jnp.where(causal, cum_decay[:, :, None] - cum_decay[:, None, :], 0.0)
    mask_mat = jnp.where(causal, jnp.exp(gap_decay), 0.0)
    grad_scores = (contract("thd,shd->hts", grad_blk, value_blk) * mask_mat).astype(jnp.bfloat16)
    attn_scores = (contract("thd,shd->hts", query_blk, key_blk) * mask_mat).astype(jnp.bfloat16)
    fwd_round = enter_fwd.astype(jnp.bfloat16)
    bwd_round = enter_bwd.astype(jnp.bfloat16)
    head_decay = jnp.exp(cum_decay).T[:, :, None]
    tail_decay = jnp.exp(end_decay[:, None] - cum_decay).T[:, :, None]
    grad_query = contract("hts,shd->thd", grad_scores, key_blk) + contract("thb,hab->tha", grad_blk, fwd_round) * head_decay
    grad_key = contract("hts,thd->shd", grad_scores, query_blk) + contract("shb,hab->sha", value_blk, bwd_round) * tail_decay
    grad_value = contract("hts,thd->shd", attn_scores, grad_blk) + contract("sha,hab->shb", key_blk, bwd_round) * tail_decay
    return grad_query.astype(jnp.bfloat16), grad_key.astype(jnp.bfloat16), grad_value.astype(jnp.bfloat16)


def advance(memory, inputs):
    block_state, block_end = inputs
    return jnp.exp(block_end)[:, None, None] * memory + block_state, memory


def reference(queries, key_vectors, value_vectors, log_decay, grad_output, out_weight):
    head_grads = jnp.dot(grad_output, out_weight.T, preferred_element_type=jnp.float32).astype(jnp.bfloat16)
    blk_count = TOKEN_COUNT // BLK

    def split_rows(matrix):
        return matrix.reshape(blk_count, BLK, HEAD_COUNT, HD)

    query_blks = split_rows(queries)
    key_blks = split_rows(key_vectors)
    value_blks = split_rows(value_vectors)
    grad_blks = split_rows(head_grads)
    decay_blks = log_decay.reshape(HEAD_COUNT, blk_count, BLK).transpose(1, 0, 2)
    key_value, end_decay = lax.map(lambda inputs: key_sums(*inputs), (key_blks, value_blks, decay_blks))
    query_grad = lax.map(lambda inputs: query_sums(*inputs), (query_blks, grad_blks, decay_blks))
    zero_state = jnp.zeros((HEAD_COUNT, HD, HD), jnp.float32)
    _, enter_fwd = lax.scan(advance, zero_state, (key_value, end_decay))
    _, enter_bwd = lax.scan(advance, zero_state, (query_grad, end_decay), reverse=True)
    grad_q, grad_k, grad_v = lax.map(lambda inputs: block_terms(*inputs), (query_blks, key_blks, value_blks, grad_blks, decay_blks, enter_fwd, enter_bwd))

    def join_rows(blocks):
        return blocks.reshape(TOKEN_COUNT, HEAD_COUNT * HD)

    return (join_rows(grad_q), join_rows(grad_k), join_rows(grad_v))
```

```python
import jax
import jax.numpy as jnp
from jax import lax
from jax.experimental import pallas as pl
from jax.experimental.pallas import tpu as pltpu
from jax.sharding import PartitionSpec as P

HD = 128
BLK = 256
MESH = pl.DeviceIdType.MESH
F32 = jnp.float32
BF16 = jnp.bfloat16


def dot_nn(a, b):
    return lax.dot_general(a, b, (((1,), (0,)), ((), ())), preferred_element_type=F32)


def dot_nt(a, b):
    return lax.dot_general(a, b, (((1,), (1,)), ((), ())), preferred_element_type=F32)


def dot_tn(a, b):
    return lax.dot_general(a, b, (((0,), (0,)), ((), ())), preferred_element_type=F32)


def make_kernel(ns, tp, tok, nh, dp, blk):
    nb = tok // blk
    nc = 2 * nb
    ch = tok // nc
    own_rows = nh * HD // ns

    def kernel(
        q_hbm, k_hbm, v_hbm, ld_hbm, x_hbm, w_hbm,
        gq_hbm, gk_hbm, gv_hbm,
        xb, wb, qb, kb, vb, gb, acc, pk, pv, ldb, cumr, cumc,
        floc, fbf, bbf, bcur, sf, sb, rf, rb, of, ob, gif, gib, tot, totown,
        x_send, x_recv, w_sem, in_sem, out_sem, ld_sem,
        t_send, t_recv, f1_send, f1_recv, f2_send, f2_recv, b1_send, b1_recv, b2_send, b2_recv,
    ):
        s = lax.axis_index("seq")
        t = lax.axis_index("tp")
        c = lax.rem(t, 2)
        y = t // 2
        up = {"tp": lax.rem(t + 2, tp)}
        down = {"tp": lax.rem(t + tp - 2, tp)}
        sib = {"tp": t + 1 - 2 * c}
        far = {"tp": lax.rem(t + 2 + c * (tp - 4), tp)}
        fslot = 6 - 4 * c
        oslot = 2 + 4 * c

        def peer(i):
            return lax.rem(s + i, ns)

        def head_cols(h):
            return pl.ds(pl.multiple_of(h * HD, HD), HD)

        def in_copy(n, h):
            src = (k_hbm, v_hbm, q_hbm)[n]
            dst = (kb, vb, qb)[n]
            return pltpu.make_async_copy(src.at[:, head_cols(h)], dst.at[h], in_sem.at[n, h])

        def w_copy(r):
            dy, oc = r // 2, r % 2
            piece = lax.rem(y + dy, tp // 2) * 2 + (c if oc == 0 else 1 - c)
            cols = pl.ds(pl.multiple_of(piece * dp, HD), dp)
            return pltpu.make_async_copy(w_hbm.at[:, cols], wb.at[r], w_sem.at[r])

        ld_copy = pltpu.make_async_copy(ld_hbm, ldb, ld_sem.at[0])
        own_copy = pltpu.make_async_copy(x_hbm, xb.at[0], ld_sem.at[1])
        ld_copy.start()
        for n in range(2):
            for h in range(nh):
                in_copy(n, h).start()
        own_copy.start()
        for h in range(nh):
            in_copy(2, h).start()
        for r in range(tp):
            w_copy(r).start()

        barrier = pltpu.get_barrier_semaphore()
        for dev in (up, down, sib):
            pl.semaphore_signal(barrier, inc=1, device_id=dev, device_id_type=MESH)

        @pl.loop(1, ns)
        def _(i):
            pl.semaphore_signal(barrier, inc=1, device_id={"seq": peer(i)}, device_id_type=MESH)

        pl.semaphore_wait(barrier, 3 + ns - 1)

        def rows_of(k):
            return pl.ds((nb - 1 - k // 2) * blk + (k % 2) * ch, ch)

        def x_copy(n, k):
            rows = rows_of(k)
            if n < 3:
                src = x_hbm.at[rows, :]
                slot, dev = ((6, up), (2, down), (1, sib))[n]
            else:
                slot, dev, src_slot = (
                    (4, far, fslot), (fslot + 1, sib, fslot), (oslot + 1, sib, oslot), (5, sib, 4)
                )[n - 3]
                src = xb.at[src_slot, rows, :]
            return pltpu.make_async_remote_copy(
                src_ref=src,
                dst_ref=xb.at[slot, rows, :],
                send_sem=x_send.at[n, k],
                recv_sem=x_recv.at[slot, k],
                device_id=dev,
                device_id_type=MESH,
            )

        def x_wait(slot, k):
            rows = rows_of(k)
            pltpu.make_async_remote_copy(
                src_ref=xb.at[slot, rows, :],
                dst_ref=xb.at[slot, rows, :],
                send_sem=x_send.at[0, k],
                recv_sem=x_recv.at[slot, k],
                device_id=sib,
                device_id_type=MESH,
            ).wait_recv()

        def own_send(k):
            if k < nc:
                for n in range(3):
                    x_copy(n, k).start()

        def relay_near(k):
            x_wait(fslot, k)
            x_copy(3, k).start()
            x_copy(4, k).start()
            own_send(k + 2)
            x_wait(oslot, k)
            x_copy(5, k).start()

        def relay_far(k):
            x_wait(4, k)
            x_copy(6, k).start()

        own_send(0)
        own_send(1)

        ld_copy.wait()
        row_i = lax.broadcasted_iota(jnp.int32, (blk, blk), 0)
        col_i = lax.broadcasted_iota(jnp.int32, (blk, blk), 1)
        tri = jnp.where(col_i <= row_i, 1.0, 0.0).astype(F32)
        for j in range(nb):
            part = ldb[:, j * blk:(j + 1) * blk]
            dims = (((1,), (1,)), ((), ()))
            cumr[:, j * blk:(j + 1) * blk] = lax.dot_general(
                part, tri, dims, precision=lax.Precision.HIGHEST, preferred_element_type=F32
            )
            col = lax.dot_general(
                tri, part, dims, precision=lax.Precision.HIGHEST, preferred_element_type=F32
            )
            for h in range(nh):
                cumc[h, j * blk:(j + 1) * blk, :] = jnp.broadcast_to(col[:, h:h + 1], (blk, HD))

        def end_of(j, h):
            return cumc[h, pl.ds(j * blk + blk - 1, 1), :]

        for h in range(nh):
            total = end_of(0, h)
            for j in range(1, nb):
                total = total + end_of(j, h)
            totown[h:h + 1, :] = total
        tot[s] = totown[...]

        def exchange(i, src, dst, send, recv, device):
            return pltpu.make_async_remote_copy(
                src_ref=src, dst_ref=dst, send_sem=send.at[i], recv_sem=recv,
                device_id={"seq": device}, device_id_type=MESH,
            )

        def state_rows(d):
            return pl.ds(pl.multiple_of(d * own_rows, own_rows), own_rows)

        def tot_copy(i):
            return exchange(i, totown, tot.at[s], t_send, t_recv.at[s], peer(i))

        def tot_in(i):
            return exchange(i, totown, tot.at[peer(i)], t_send, t_recv.at[peer(i)], peer(i))

        def first_copy(i, st, rx, send, recv):
            return exchange(i, st.at[state_rows(peer(i)), :], rx.at[s], send, recv.at[s], peer(i))

        def first_in(i, st, rx, send, recv):
            d = peer(i)
            return exchange(i, st.at[state_rows(d), :], rx.at[d], send, recv.at[d], d)

        def second_copy(i, out, gi, send, recv):
            return exchange(i, out.at[peer(i)], gi.at[state_rows(s), :], send, recv.at[s], peer(i))

        def second_in(i, out, gi, send, recv):
            d = peer(i)
            return exchange(i, out.at[d], gi.at[state_rows(d), :], send, recv.at[d], d)

        @pl.loop(1, ns)
        def _(i):
            tot_copy(i).start()

        for h in range(nh):
            in_copy(0, h).wait()
            in_copy(1, h).wait()

        @pl.loop(0, nh)
        def _(h):
            state = jnp.zeros((HD, HD), F32)
            for j in range(nb):
                rows = pl.ds(j * blk, blk)
                floc[j, h] = state
                weight = jnp.exp(end_of(j, h) - cumc[h, rows, :])
                scaled = (kb[h, rows, :] * weight).astype(BF16)
                state = jnp.exp(end_of(j, h)) * state + dot_tn(scaled, vb[h, rows, :])
            sf[pl.ds(pl.multiple_of(h * HD, HD), HD), :] = state.astype(BF16)

        @pl.loop(1, ns)
        def _(i):
            first_copy(i, sf, rf, f1_send, f1_recv).start()

        rf[s] = sf[state_rows(s), :]

        my_head = (s * own_rows) // HD

        def combine(rx, out, gi, order, src, send, recv):
            @pl.loop(1, ns)
            def _(i):
                first_in(i, src, rx, *recv).wait_recv()

            state = jnp.zeros((own_rows, HD), F32)
            for d in order:
                out[d] = state.astype(BF16)
                state = jnp.exp(tot[d, pl.ds(my_head, 1), :]) * state + rx[d].astype(F32)

            @pl.loop(1, ns)
            def _(i):
                second_copy(i, out, gi, *send).start()

            gi[state_rows(s), :] = out[s]

        def project(b, slots):
            rows = pl.ds((nb - 1 - b) * blk, blk)

            @pl.loop(slots[0], slots[1])
            def _(r):
                acc[...] += dot_nt(xb[r, rows, :], wb[r])

        def arrived(b, slots):
            for r in slots:
                for k in (2 * b, 2 * b + 1):
                    x_wait(r, k)

        def query_sums(b):
            j = nb - 1 - b
            rows = pl.ds(j * blk, blk)
            for h in range(nh):
                gb[h, rows, :] = acc[:, h * HD:(h + 1) * HD].astype(BF16)

            @pl.loop(0, nh)
            def _(h):
                weight = jnp.exp(cumc[h, rows, :])
                scaled = (qb[h, rows, :] * weight).astype(BF16)
                total = dot_tn(scaled, gb[h, rows, :])
                if b == 0:
                    bbf[j, h] = jnp.zeros((HD, HD), BF16)
                    bcur[h] = total
                else:
                    held = bcur[h]
                    bbf[j, h] = held.astype(BF16)
                    bcur[h] = jnp.exp(end_of(j, h)) * held + total

        def block_terms(b):
            j = nb - 1 - b
            rows = pl.ds(j * blk, blk)

            @pl.loop(0, nh)
            def _(h):
                qm, km, vm, gm = qb[h, rows, :], kb[h, rows, :], vb[h, rows, :], gb[h, rows, :]
                cum = cumc[h, rows, :]
                cum_wide = jnp.concatenate([cum] * (blk // HD), axis=1)
                gap = cumr[pl.ds(h, 1), rows] - cum_wide
                later = lax.broadcasted_iota(jnp.int32, (blk, blk), 1) >= lax.broadcasted_iota(
                    jnp.int32, (blk, blk), 0
                )
                mask = jnp.where(later, jnp.exp(gap), 0.0)
                gs = (dot_nt(vm, gm) * mask).astype(BF16)
                at = (dot_nt(km, qm) * mask).astype(BF16)
                tail = jnp.exp(end_of(j, h) - cum)
                bw = bbf[j, h]
                pk[h, rows, :] = dot_nn(gs, qm) + dot_nt(vm, bw) * tail
                pv[h, rows, :] = dot_nn(at, gm) + dot_nn(km, bw) * tail
                gq = dot_tn(gs, km) + dot_nt(gm, fbf[j, h]) * jnp.exp(cum)
                qb[h, rows, :] = gq.astype(BF16)

        def gq_copy(h):
            return pltpu.make_async_copy(qb.at[h], gq_hbm.at[:, head_cols(h)], out_sem.at[0, h])

        def gk_copy(h):
            return pltpu.make_async_copy(kb.at[h], gk_hbm.at[:, head_cols(h)], out_sem.at[1, h])

        def gv_copy(h):
            return pltpu.make_async_copy(vb.at[h], gv_hbm.at[:, head_cols(h)], out_sem.at[2, h])

        f_args = ((f2_send, f2_recv), (f1_send, f1_recv))
        b_args = ((b2_send, b2_recv), (b1_send, b1_recv))

        relay_near(0)
        own_copy.wait()
        for h in range(nh):
            in_copy(2, h).wait()
        relay_near(1)
        relay_far(0)

        @pl.loop(1, ns)
        def _(i):
            tot_in(i).wait_recv()

        combine(rf, of, gif, range(ns), sf, *f_args)
        for r in range(tp):
            w_copy(r).wait()

        for b in range(nb):
            acc[...] = jnp.zeros_like(acc)
            last = b == nb - 1
            if not last:
                relay_near(2 * b + 2)
            relay_far(2 * b + 1)
            if last:
                arrived(b, (1, 3))
                project(b, (0, 4))
                arrived(b, (7,))
                project(b, (6, 8))
                project(b, (4, 5))
                arrived(b, (5,))
                project(b, (5, 6))
            else:
                arrived(b, (1, 3, 5, 7))
                project(b, (0, 8))
            query_sums(b)
            if b == 0:
                @pl.loop(1, ns)
                def _(i):
                    second_in(i, of, gif, f2_send, f2_recv).wait_recv()

                @pl.loop(0, nh)
                def _(h):
                    entry = gif[pl.ds(pl.multiple_of(h * HD, HD), HD), :].astype(F32)
                    prior = jnp.zeros((1, HD), F32)
                    for j in range(nb):
                        fbf[j, h] = (floc[j, h] + jnp.exp(prior) * entry).astype(BF16)
                        prior = prior + end_of(j, h)
            if last:
                @pl.loop(0, nh)
                def _(h):
                    sb[pl.ds(pl.multiple_of(h * HD, HD), HD), :] = bcur[h].astype(BF16)

                @pl.loop(1, ns)
                def _(i):
                    first_copy(i, sb, rb, b1_send, b1_recv).start()

                rb[s] = sb[state_rows(s), :]
            else:
                relay_near(2 * b + 3)
                relay_far(2 * b + 2)
            block_terms(b)

        @pl.loop(0, nh)
        def _(h):
            gq_copy(h).start()

        combine(rb, ob, gib, range(ns - 1, -1, -1), sb, *b_args)

        @pl.loop(1, ns)
        def _(i):
            second_in(i, ob, gib, b2_send, b2_recv).wait_recv()

        @pl.loop(0, nh)
        def _(h):
            entry = gib[pl.ds(pl.multiple_of(h * HD, HD), HD), :]
            after = jnp.zeros((1, HD), F32)
            for j in range(nb - 1, -1, -1):
                rows = pl.ds(j * blk, blk)
                after = after + end_of(j, h)
                tail = jnp.exp(after - cumc[h, rows, :])
                km, vm = kb[h, rows, :], vb[h, rows, :]
                kb[h, rows, :] = (pk[h, rows, :] + dot_nt(vm, entry) * tail).astype(BF16)
                vb[h, rows, :] = (pv[h, rows, :] + dot_nn(km, entry) * tail).astype(BF16)
            gk_copy(h).start()
            gv_copy(h).start()

        for k in range(nc):
            for n in range(7):
                x_copy(n, k).wait_send()

        @pl.loop(1, ns)
        def _(i):
            tot_copy(i).wait_send()
            first_copy(i, sf, rf, f1_send, f1_recv).wait_send()
            second_copy(i, of, gif, f2_send, f2_recv).wait_send()
            first_copy(i, sb, rb, b1_send, b1_recv).wait_send()
            second_copy(i, ob, gib, b2_send, b2_recv).wait_send()

        @pl.loop(0, nh)
        def _(h):
            gq_copy(h).wait()
            gk_copy(h).wait()
            gv_copy(h).wait()

    dma = pltpu.SemaphoreType.DMA
    scratch = [
        pltpu.VMEM((tp, tok, dp), BF16),
        pltpu.VMEM((tp, nh * HD, dp), BF16),
        pltpu.VMEM((nh, tok, HD), BF16),
        pltpu.VMEM((nh, tok, HD), BF16),
        pltpu.VMEM((nh, tok, HD), BF16),
        pltpu.VMEM((nh, tok, HD), BF16),
        pltpu.VMEM((blk, nh * HD), F32),
        pltpu.VMEM((nh, tok, HD), F32),
        pltpu.VMEM((nh, tok, HD), F32),
        pltpu.VMEM((nh, tok), F32),
        pltpu.VMEM((nh, tok), F32),
        pltpu.VMEM((nh, tok, HD), F32),
        pltpu.VMEM((nb, nh, HD, HD), F32),
        pltpu.VMEM((nb, nh, HD, HD), BF16),
        pltpu.VMEM((nb, nh, HD, HD), BF16),
        pltpu.VMEM((nh, HD, HD), F32),
        pltpu.VMEM((nh * HD, HD), BF16),
        pltpu.VMEM((nh * HD, HD), BF16),
        pltpu.VMEM((ns, own_rows, HD), BF16),
        pltpu.VMEM((ns, own_rows, HD), BF16),
        pltpu.VMEM((ns, own_rows, HD), BF16),
        pltpu.VMEM((ns, own_rows, HD), BF16),
        pltpu.VMEM((nh * HD, HD), BF16),
        pltpu.VMEM((nh * HD, HD), BF16),
        pltpu.VMEM((ns, nh, HD), F32),
        pltpu.VMEM((nh, HD), F32),
        dma((7, nc)),
        dma((tp, nc)),
        dma((tp,)),
        dma((3, nh)),
        dma((3, nh)),
        dma((2,)),
    ] + [dma((ns,))] * 10
    out = jax.ShapeDtypeStruct((tok, nh * HD), BF16)
    hbm = pl.BlockSpec(memory_space=pl.ANY)
    return pl.pallas_call(
        kernel,
        out_shape=(out, out, out),
        in_specs=[hbm] * 6,
        out_specs=(hbm, hbm, hbm),
        scratch_shapes=scratch,
        compiler_params=pltpu.CompilerParams(
            collective_id=0, has_side_effects=True, vmem_limit_bytes=65000000
        ),
    )


def solution(mesh, blk=BLK):
    ns, tp = mesh.shape["seq"], mesh.shape["tp"]

    def local(queries, key_vectors, value_vectors, log_decay, grad_output, out_weight):
        tok, width = queries.shape
        call = make_kernel(ns, tp, tok, width // HD, grad_output.shape[1], blk)
        return call(queries, key_vectors, value_vectors, log_decay, grad_output, out_weight)

    in_specs = (
        P("seq", "tp"),
        P("seq", "tp"),
        P("seq", "tp"),
        P("tp", "seq"),
        P("seq", "tp"),
        P("tp", None),
    )
    out_specs = (P("seq", "tp"), P("seq", "tp"), P("seq", "tp"))
    return jax.shard_map(local, mesh=mesh, in_specs=in_specs, out_specs=out_specs, check_vma=False)
```

```python
import jax
import jax.numpy as jnp
from jax import lax
from jax.experimental import pallas as pl
from jax.experimental.pallas import tpu as pltpu
from jax.sharding import PartitionSpec as P

HD = 128
BLK = 256
MESH = pl.DeviceIdType.MESH
F32 = jnp.float32
BF16 = jnp.bfloat16
VMEM_FIRST = 45000000
VMEM_SECOND = 8000000


def dot_nn(a, b):
    return lax.dot_general(a, b, (((1,), (0,)), ((), ())), preferred_element_type=F32)


def dot_nt(a, b):
    return lax.dot_general(a, b, (((1,), (1,)), ((), ())), preferred_element_type=F32)


def dot_tn(a, b):
    return lax.dot_general(a, b, (((0,), (0,)), ((), ())), preferred_element_type=F32)


def make_kernel(ns, tp, tok, nh, dp, blk):
    nb = tok // blk
    nc = 2 * nb
    ch = tok // nc
    owners = ns // nh
    own_rows = nh * HD // ns

    def kernel(
        q_hbm, k_hbm, v_hbm, ld_hbm, x_hbm, w_hbm,
        qb, kb, vb, pk, pv, cumc, gib,
        xb, wb, gb, acc, ldb, cumr,
        floc, fbf, bbf, bcur, sf, sb, rf, rb, of, ob, gif, tot, totown,
        x_send, x_recv, w_sem, in_sem, ld_sem,
        t_send, t_recv, f1_send, f1_recv, f2_send, f2_recv, b1_send, b1_recv, b2_send, b2_recv,
    ):
        s = lax.axis_index("seq")
        t = lax.axis_index("tp")
        c = lax.rem(t, 2)
        y = t // 2
        up = {"tp": lax.rem(t + 2, tp)}
        down = {"tp": lax.rem(t + tp - 2, tp)}
        sib = {"tp": t + 1 - 2 * c}
        far = {"tp": lax.rem(t + 2 + c * (tp - 4), tp)}
        fslot = 6 - 4 * c
        oslot = 2 + 4 * c

        def peer(i):
            return lax.rem(s + i, ns)

        def head_cols(h):
            return pl.ds(pl.multiple_of(h * HD, HD), HD)

        def in_copy(n, h):
            src = (k_hbm, v_hbm, q_hbm)[n]
            dst = (kb, vb, qb)[n]
            return pltpu.make_async_copy(src.at[:, head_cols(h)], dst.at[h], in_sem.at[n, h])

        def w_copy(r):
            dy, oc = r // 2, r % 2
            piece = lax.rem(y + dy, tp // 2) * 2 + (c if oc == 0 else 1 - c)
            cols = pl.ds(pl.multiple_of(piece * dp, HD), dp)
            return pltpu.make_async_copy(w_hbm.at[:, cols], wb.at[r], w_sem.at[r])

        ld_copy = pltpu.make_async_copy(ld_hbm, ldb, ld_sem.at[0])
        own_copy = pltpu.make_async_copy(x_hbm, xb.at[0], ld_sem.at[1])
        ld_copy.start()
        for n in range(2):
            for h in range(nh):
                in_copy(n, h).start()
        own_copy.start()
        for h in range(nh):
            in_copy(2, h).start()
        for r in range(tp):
            w_copy(r).start()

        barrier = pltpu.get_barrier_semaphore()
        for dev in (up, down, sib):
            pl.semaphore_signal(barrier, inc=1, device_id=dev, device_id_type=MESH)

        @pl.loop(1, ns)
        def _(i):
            pl.semaphore_signal(barrier, inc=1, device_id={"seq": peer(i)}, device_id_type=MESH)

        pl.semaphore_wait(barrier, 3 + ns - 1)

        def rows_of(k):
            return pl.ds((nb - 1 - k // 2) * blk + (k % 2) * ch, ch)

        def x_copy(n, k):
            rows = rows_of(k)
            if n < 3:
                src = x_hbm.at[rows, :]
                slot, dev = ((6, up), (2, down), (1, sib))[n]
            else:
                slot, dev, held = (
                    (4, far, fslot), (fslot + 1, sib, fslot), (oslot + 1, sib, oslot), (5, sib, 4)
                )[n - 3]
                src = xb.at[held, rows, :]
            return pltpu.make_async_remote_copy(
                src_ref=src,
                dst_ref=xb.at[slot, rows, :],
                send_sem=x_send.at[n, k],
                recv_sem=x_recv.at[slot, k],
                device_id=dev,
                device_id_type=MESH,
            )

        def x_wait(slot, k):
            rows = rows_of(k)
            pltpu.make_async_remote_copy(
                src_ref=xb.at[slot, rows, :],
                dst_ref=xb.at[slot, rows, :],
                send_sem=x_send.at[0, k],
                recv_sem=x_recv.at[slot, k],
                device_id=sib,
                device_id_type=MESH,
            ).wait_recv()

        def near(k):
            x_wait(fslot, k)
            x_copy(3, k).start()
            x_copy(4, k).start()
            x_wait(oslot, k)
            x_copy(5, k).start()

        def distant(k):
            x_wait(4, k)
            x_copy(6, k).start()

        for k in range(nc):
            for n in range(3):
                x_copy(n, k).start()

        ld_copy.wait()
        row_i = lax.broadcasted_iota(jnp.int32, (blk, blk), 0)
        col_i = lax.broadcasted_iota(jnp.int32, (blk, blk), 1)
        tri = jnp.where(col_i <= row_i, 1.0, 0.0).astype(F32)
        for j in range(nb):
            part = ldb[:, j * blk:(j + 1) * blk]
            dims = (((1,), (1,)), ((), ()))
            cumr[:, j * blk:(j + 1) * blk] = lax.dot_general(
                part, tri, dims, precision=lax.Precision.HIGHEST, preferred_element_type=F32
            )
            col = lax.dot_general(
                tri, part, dims, precision=lax.Precision.HIGHEST, preferred_element_type=F32
            )
            for h in range(nh):
                cumc[h, j * blk:(j + 1) * blk, :] = jnp.broadcast_to(col[:, h:h + 1], (blk, HD))

        def end_of(j, h):
            return cumc[h, pl.ds(j * blk + blk - 1, 1), :]

        for h in range(nh):
            total = end_of(0, h)
            for j in range(1, nb):
                total = total + end_of(j, h)
            totown[h:h + 1, :] = total
        tot[s] = totown[...]

        def exchange(i, src, dst, send, recv, device):
            return pltpu.make_async_remote_copy(
                src_ref=src, dst_ref=dst, send_sem=send.at[i], recv_sem=recv,
                device_id={"seq": device}, device_id_type=MESH,
            )

        def state_rows(d):
            return pl.ds(pl.multiple_of(d * own_rows, own_rows), own_rows)

        def tot_copy(i):
            return exchange(i, totown, tot.at[s], t_send, t_recv.at[s], peer(i))

        def tot_in(i):
            return exchange(i, totown, tot.at[peer(i)], t_send, t_recv.at[peer(i)], peer(i))

        def first_copy(o, st, rx, send, recv):
            return exchange(o, st.at[state_rows(o), :], rx.at[s], send, recv.at[s], o)

        def first_in(d, st, rx, send, recv):
            return exchange(d, st.at[state_rows(d), :], rx.at[d], send, recv.at[d], d)

        def second_copy(o, out, gi, send, recv):
            return exchange(o, out.at[o], gi.at[state_rows(s), :], send, recv.at[s], o)

        def second_in(d, out, gi, send, recv):
            return exchange(d, out.at[d], gi.at[state_rows(d), :], send, recv.at[d], d)

        def send_head(h, state, st, rx, send, recv):
            st[pl.ds(pl.multiple_of(h * HD, HD), HD), :] = state.astype(BF16)
            for n in range(owners):
                o = h * owners + n

                @pl.when(o != s)
                def _():
                    first_copy(o, st, rx, send, recv).start()

        @pl.loop(1, ns)
        def _(i):
            tot_copy(i).start()

        for h in range(nh):
            in_copy(0, h).wait()
            in_copy(1, h).wait()

        @pl.loop(0, nh)
        def _(h):
            state = jnp.zeros((HD, HD), F32)
            for j in range(nb):
                rows = pl.ds(j * blk, blk)
                floc[j, h] = state
                weight = jnp.exp(end_of(j, h) - cumc[h, rows, :])
                scaled = (kb[h, rows, :] * weight).astype(BF16)
                state = jnp.exp(end_of(j, h)) * state + dot_tn(scaled, vb[h, rows, :])
            send_head(h, state, sf, rf, f1_send, f1_recv)

        rf[s] = sf[state_rows(s), :]

        my_head = (s * own_rows) // HD

        def combine(st, rx, out, gi, order, first, second):
            state = jnp.zeros((own_rows, HD), F32)
            for d in order:
                out[d] = state.astype(BF16)

                @pl.when(d != s)
                def _():
                    second_copy(d, out, gi, *second).start()
                    first_in(d, st, rx, *first).wait_recv()

                state = jnp.exp(tot[d, pl.ds(my_head, 1), :]) * state + rx[d].astype(F32)

            gi[state_rows(s), :] = out[s]

        def entry_wait(d, out, gi, second):
            @pl.when(d != s)
            def _():
                second_in(d, out, gi, *second).wait_recv()

        def project(chunks, slots, init=False):
            base = (nb - 1 - chunks[0] // 2) * blk + (chunks[0] % 2) * ch
            rows = pl.ds(base, len(chunks) * ch)

            if init:
                acc[rows, :] = dot_nt(xb[slots[0], rows, :], wb[slots[0]])

            @pl.loop(slots[0] + (1 if init else 0), slots[1])
            def _(r):
                acc[rows, :] += dot_nt(xb[r, rows, :], wb[r])

        def arrived(chunks, slots):
            for k in chunks:
                for r in slots:
                    x_wait(r, k)

        def query_sums(b):
            j = nb - 1 - b
            rows = pl.ds(j * blk, blk)
            for h in range(nh):
                gb[h, rows, :] = acc[rows, h * HD:(h + 1) * HD].astype(BF16)

            @pl.loop(0, nh)
            def _(h):
                weight = jnp.exp(cumc[h, rows, :])
                scaled = (qb[h, rows, :] * weight).astype(BF16)
                total = dot_tn(scaled, gb[h, rows, :])
                if b == 0:
                    bbf[j, h] = jnp.zeros((HD, HD), BF16)
                else:
                    held = bcur[h]
                    bbf[j, h] = held.astype(BF16)
                    total = jnp.exp(end_of(j, h)) * held + total
                if b == nb - 1:
                    send_head(h, total, sb, rb, b1_send, b1_recv)
                else:
                    bcur[h] = total

        def block_terms(b):
            j = nb - 1 - b
            rows = pl.ds(j * blk, blk)

            @pl.loop(0, nh)
            def _(h):
                qm, km, vm, gm = qb[h, rows, :], kb[h, rows, :], vb[h, rows, :], gb[h, rows, :]
                cum = cumc[h, rows, :]
                cum_wide = jnp.concatenate([cum] * (blk // HD), axis=1)
                gap = cumr[pl.ds(h, 1), rows] - cum_wide
                later = lax.broadcasted_iota(jnp.int32, (blk, blk), 1) >= lax.broadcasted_iota(
                    jnp.int32, (blk, blk), 0
                )
                mask = jnp.where(later, jnp.exp(gap), 0.0)
                gs = (dot_nt(vm, gm) * mask).astype(BF16)
                at = (dot_nt(km, qm) * mask).astype(BF16)
                tail = jnp.exp(end_of(j, h) - cum)
                bw = bbf[j, h]
                pk[h, rows, :] = dot_nn(gs, qm) + dot_nt(vm, bw) * tail
                pv[h, rows, :] = dot_nn(at, gm) + dot_nn(km, bw) * tail
                gq = dot_tn(gs, km) + dot_nt(gm, fbf[j, h]) * jnp.exp(cum)
                qb[h, rows, :] = gq.astype(BF16)

        fwd = ((f1_send, f1_recv), (f2_send, f2_recv))
        bwd = ((b1_send, b1_recv), (b2_send, b2_recv))

        def near_terms(b):
            pair = (2 * b, 2 * b + 1)
            arrived(pair, (1, 3, 7))
            project(pair, (0, 4), init=True)
            project(pair, (6, 8))

        near(0)

        @pl.loop(1, ns)
        def _(i):
            tot_in(i).wait_recv()

        combine(sf, rf, of, gif, range(ns), *fwd)
        near(1)
        own_copy.wait()
        for h in range(nh):
            in_copy(2, h).wait()
        for r in range(tp):
            w_copy(r).wait()

        for b in range(nb):
            if b > 0:
                near(2 * b)
                near(2 * b + 1)
            if b == 1:
                for d in range(ns):
                    entry_wait(d, of, gif, fwd[1])

                @pl.loop(0, nh)
                def _(h):
                    entry = gif[pl.ds(pl.multiple_of(h * HD, HD), HD), :].astype(F32)
                    prior = jnp.zeros((1, HD), F32)
                    for j in range(nb):
                        fbf[j, h] = (floc[j, h] + jnp.exp(prior) * entry).astype(BF16)
                        prior = prior + end_of(j, h)
            near_terms(b)

        distant(0)
        distant(1)
        for b in range(nb):
            pair = (2 * b, 2 * b + 1)
            if b < nb - 1:
                arrived(pair, (5,))
                project(pair, (4, 6))
                query_sums(b)
                distant(2 * b + 2)
                if b < nb - 2:
                    distant(2 * b + 3)
                if b == 0:
                    block_terms(b)
            else:
                arrived(pair[:1], (5,))
                project(pair[:1], (4, 6))
                distant(pair[1])
                project(pair[1:], (4, 5))
                arrived(pair[1:], (5,))
                project(pair[1:], (5, 6))
                query_sums(b)
        rb[s] = sb[state_rows(s), :]
        for b in range(1, nb - 1):
            block_terms(b)
        combine(sb, rb, ob, gib, range(ns - 1, -1, -1), *bwd)
        block_terms(nb - 1)
        for d in range(ns):
            entry_wait(d, ob, gib, bwd[1])

        for k in range(nc):
            for n in range(7):
                x_copy(n, k).wait_send()

        @pl.loop(1, ns)
        def _(i):
            tot_copy(i).wait_send()
            d = peer(i)
            first_copy(d, sf, rf, f1_send, f1_recv).wait_send()
            second_copy(d, of, gif, f2_send, f2_recv).wait_send()
            first_copy(d, sb, rb, b1_send, b1_recv).wait_send()
            second_copy(d, ob, gib, b2_send, b2_recv).wait_send()

    dma = pltpu.SemaphoreType.DMA
    scratch = [
        pltpu.VMEM((tp, tok, dp), BF16),
        pltpu.VMEM((tp, nh * HD, dp), BF16),
        pltpu.VMEM((nh, tok, HD), BF16),
        pltpu.VMEM((tok, nh * HD), F32),
        pltpu.VMEM((nh, tok), F32),
        pltpu.VMEM((nh, tok), F32),
        pltpu.VMEM((nb, nh, HD, HD), F32),
        pltpu.VMEM((nb, nh, HD, HD), BF16),
        pltpu.VMEM((nb, nh, HD, HD), BF16),
        pltpu.VMEM((nh, HD, HD), F32),
        pltpu.VMEM((nh * HD, HD), BF16),
        pltpu.VMEM((nh * HD, HD), BF16),
        pltpu.VMEM((ns, own_rows, HD), BF16),
        pltpu.VMEM((ns, own_rows, HD), BF16),
        pltpu.VMEM((ns, own_rows, HD), BF16),
        pltpu.VMEM((ns, own_rows, HD), BF16),
        pltpu.VMEM((nh * HD, HD), BF16),
        pltpu.VMEM((ns, nh, HD), F32),
        pltpu.VMEM((nh, HD), F32),
        dma((7, nc)),
        dma((tp, nc)),
        dma((tp,)),
        dma((3, nh)),
        dma((2,)),
    ] + [dma((ns,))] * 10
    hbm = pl.BlockSpec(memory_space=pl.ANY)
    vmem = pl.BlockSpec(memory_space=pltpu.VMEM)
    heads = (nh, tok, HD)
    held = [(heads, BF16)] * 3 + [(heads, F32)] * 3 + [((nh * HD, HD), BF16)]
    first = pl.pallas_call(
        kernel,
        out_shape=tuple(pltpu.VMEM(*one) for one in held),
        in_specs=[hbm] * 6,
        out_specs=(vmem,) * len(held),
        scratch_shapes=scratch,
        compiler_params=pltpu.CompilerParams(
            collective_id=0, has_side_effects=True, vmem_limit_bytes=VMEM_FIRST
        ),
    )

    def finish(qb, kb, vb, pk, pv, cumc, gib, gq_hbm, gk_hbm, gv_hbm, kout, vout, out_sem):
        def out_copy(n, h):
            cols = pl.ds(pl.multiple_of(h * HD, HD), HD)
            src, dst = ((qb, gq_hbm), (kout, gk_hbm), (vout, gv_hbm))[n]
            return pltpu.make_async_copy(src.at[h], dst.at[:, cols], out_sem.at[n, h])

        @pl.loop(0, nh)
        def _(h):
            out_copy(0, h).start()
            entry = gib[pl.ds(pl.multiple_of(h * HD, HD), HD), :]
            after = jnp.zeros((1, HD), F32)
            for j in range(nb - 1, -1, -1):
                rows = pl.ds(j * blk, blk)
                after = after + cumc[h, pl.ds(j * blk + blk - 1, 1), :]
                tail = jnp.exp(after - cumc[h, rows, :])
                kout[h, rows, :] = (pk[h, rows, :] + dot_nt(vb[h, rows, :], entry) * tail).astype(BF16)
                vout[h, rows, :] = (pv[h, rows, :] + dot_nn(kb[h, rows, :], entry) * tail).astype(BF16)
            out_copy(1, h).start()
            out_copy(2, h).start()

        @pl.loop(0, nh)
        def _(h):
            for n in range(3):
                out_copy(n, h).wait()

    out = jax.ShapeDtypeStruct((tok, nh * HD), BF16)
    second = pl.pallas_call(
        finish,
        out_shape=(out, out, out),
        in_specs=[vmem] * len(held),
        out_specs=(hbm, hbm, hbm),
        scratch_shapes=[pltpu.VMEM(heads, BF16), pltpu.VMEM(heads, BF16), dma((3, nh))],
        compiler_params=pltpu.CompilerParams(vmem_limit_bytes=VMEM_SECOND),
    )

    def both(*args):
        kept = first(*args)
        return second(*(pltpu.with_memory_space_constraint(one, pltpu.VMEM) for one in kept))

    return both


def solution(mesh, blk=BLK):
    ns, tp = mesh.shape["seq"], mesh.shape["tp"]

    def local(queries, key_vectors, value_vectors, log_decay, grad_output, out_weight):
        tok, width = queries.shape
        call = make_kernel(ns, tp, tok, width // HD, grad_output.shape[1], blk)
        return call(queries, key_vectors, value_vectors, log_decay, grad_output, out_weight)

    in_specs = (
        P("seq", "tp"),
        P("seq", "tp"),
        P("seq", "tp"),
        P("tp", "seq"),
        P("seq", "tp"),
        P("tp", None),
    )
    out_specs = (P("seq", "tp"), P("seq", "tp"), P("seq", "tp"))
    return jax.shard_map(local, mesh=mesh, in_specs=in_specs, out_specs=out_specs, check_vma=False)
```

```python
import jax
import jax.numpy as jnp
from jax import lax
from jax.experimental import pallas as pl
from jax.experimental.pallas import tpu as pltpu
from jax.sharding import PartitionSpec as P

HD = 128
BLK = 256
MESH = pl.DeviceIdType.MESH
F32 = jnp.float32
BF16 = jnp.bfloat16
VMEM_FIRST = 45000000
VMEM_SECOND = 8000000
GROUP = 4
KV_GROUP = 2
LAST_GROUP = 2


def dot_nn(a, b):
    return lax.dot_general(a, b, (((1,), (0,)), ((), ())), preferred_element_type=F32)


def dot_nt(a, b):
    return lax.dot_general(a, b, (((1,), (1,)), ((), ())), preferred_element_type=F32)


def dot_tn(a, b):
    return lax.dot_general(a, b, (((0,), (0,)), ((), ())), preferred_element_type=F32)


def over_heads(nh, load, work, store, group=GROUP):
    group = min(group, nh)

    @pl.loop(0, nh // group)
    def _(i):
        heads = [i * group + n for n in range(group)]
        done = [work(h, *one) for h, one in zip(heads, [load(h) for h in heads])]
        for h, one in zip(heads, done):
            store(h, *one)


def make_kernel(ns, tp, tok, nh, dp, blk):
    nb = tok // blk
    nc = 2 * nb
    ch = tok // nc
    owners = ns // nh
    own_rows = nh * HD // ns

    def kernel(
        q_hbm, k_hbm, v_hbm, ld_hbm, x_hbm, w_hbm,
        qb, kb, vb, pk, pv, cumc, gib,
        xb, wb, gb, acc, ldb, cumr,
        floc, fbf, bbf, bcur, sf, sb, rf, rb, of, ob, gif, tot, totown, factor,
        x_send, x_recv, w_sem, in_sem, ld_sem,
        hello, t_send, t_recv, f1_send, f1_recv, f2_send, f2_recv, b1_send, b1_recv, b2_send, b2_recv,
    ):
        s = lax.axis_index("seq")
        t = lax.axis_index("tp")
        c = lax.rem(t, 2)
        y = t // 2
        up = {"tp": lax.rem(t + 2, tp)}
        down = {"tp": lax.rem(t + tp - 2, tp)}
        sib = {"tp": t + 1 - 2 * c}
        far = {"tp": lax.rem(t + 2 + c * (tp - 4), tp)}
        fslot = 6 - 4 * c
        oslot = 2 + 4 * c

        def peer(i):
            return lax.rem(s + i, ns)

        def head_cols(h):
            return pl.ds(pl.multiple_of(h * HD, HD), HD)

        def in_copy(n, h):
            src = (k_hbm, v_hbm, q_hbm)[n]
            dst = (kb, vb, qb)[n]
            return pltpu.make_async_copy(src.at[:, head_cols(h)], dst.at[h], in_sem.at[n, h])

        def w_copy(r):
            dy, oc = r // 2, r % 2
            piece = lax.rem(y + dy, tp // 2) * 2 + (c if oc == 0 else 1 - c)
            cols = pl.ds(pl.multiple_of(piece * dp, HD), dp)
            return pltpu.make_async_copy(w_hbm.at[:, cols], wb.at[r], w_sem.at[r])

        ld_copy = pltpu.make_async_copy(ld_hbm, ldb, ld_sem.at[0])
        own_copy = pltpu.make_async_copy(x_hbm, xb.at[0], ld_sem.at[1])
        ld_copy.start()
        for n in range(2):
            for h in range(nh):
                in_copy(n, h).start()
        own_copy.start()
        for h in range(nh):
            in_copy(2, h).start()
        for r in range(tp):
            w_copy(r).start()

        inner = 4 if ns % 4 == 0 else ns
        outer = ns // inner
        across, along = s // inner, lax.rem(s, inner)
        beside = []
        for step in (1, inner - 1):
            beside.append({"seq": across * inner + lax.rem(along + step, inner)})
        if outer > 1:
            for step in (1, outer - 1):
                beside.append({"seq": lax.rem(across + step, outer) * inner + along})
        rounds = inner // 2 + outer // 2

        def greet(sem, devices):
            for dev in devices:
                pl.semaphore_signal(sem, inc=1, device_id=dev, device_id_type=MESH)

        barrier = pltpu.get_barrier_semaphore()
        greet(barrier, [up, down, sib] + beside)
        pl.semaphore_wait(barrier, 3 + len(beside))

        def greet_next(r):
            if r < rounds:
                greet(hello.at[r], beside)

        def greeted(r):
            if r < rounds:
                pl.semaphore_wait(hello.at[r], len(beside))

        def rows_of(k):
            return pl.ds((nb - 1 - k // 2) * blk + (k % 2) * ch, ch)

        def x_copy(n, k):
            rows = rows_of(k)
            if n < 3:
                src = x_hbm.at[rows, :]
                slot, dev = ((6, up), (2, down), (1, sib))[n]
            else:
                slot, dev, held = (
                    (4, far, fslot), (fslot + 1, sib, fslot), (oslot + 1, sib, oslot), (5, sib, 4)
                )[n - 3]
                src = xb.at[held, rows, :]
            return pltpu.make_async_remote_copy(
                src_ref=src,
                dst_ref=xb.at[slot, rows, :],
                send_sem=x_send.at[n, k],
                recv_sem=x_recv.at[slot, k],
                device_id=dev,
                device_id_type=MESH,
            )

        def x_wait(slot, k):
            rows = rows_of(k)
            pltpu.make_async_remote_copy(
                src_ref=xb.at[slot, rows, :],
                dst_ref=xb.at[slot, rows, :],
                send_sem=x_send.at[0, k],
                recv_sem=x_recv.at[slot, k],
                device_id=sib,
                device_id_type=MESH,
            ).wait_recv()

        def near(k):
            x_wait(fslot, k)
            x_copy(3, k).start()
            x_copy(4, k).start()
            x_wait(oslot, k)
            x_copy(5, k).start()

        def distant(k):
            x_wait(4, k)
            x_copy(6, k).start()

        for k in range(nc):
            for n in range(3):
                x_copy(n, k).start()

        greet_next(1)

        ld_copy.wait()
        greeted(1)
        greet_next(2)
        row_i = lax.broadcasted_iota(jnp.int32, (blk, blk), 0)
        col_i = lax.broadcasted_iota(jnp.int32, (blk, blk), 1)
        tri = jnp.where(col_i <= row_i, 1.0, 0.0).astype(F32)
        for j in range(nb):
            part = ldb[:, j * blk:(j + 1) * blk]
            dims = (((1,), (1,)), ((), ()))
            cumr[:, j * blk:(j + 1) * blk] = lax.dot_general(
                part, tri, dims, precision=lax.Precision.HIGHEST, preferred_element_type=F32
            )
            col = lax.dot_general(
                tri, part, dims, precision=lax.Precision.HIGHEST, preferred_element_type=F32
            )
            for h in range(nh):
                cumc[h, j * blk:(j + 1) * blk, :] = jnp.broadcast_to(col[:, h:h + 1], (blk, HD))

        greeted(2)
        greet_next(3)

        def end_of(j, h):
            return cumc[h, pl.ds(j * blk + blk - 1, 1), :]

        for h in range(nh):
            total = end_of(0, h)
            for j in range(1, nb):
                total = total + end_of(j, h)
            totown[h:h + 1, :] = total
        tot[s] = totown[...]

        def exchange(i, src, dst, send, recv, device):
            return pltpu.make_async_remote_copy(
                src_ref=src, dst_ref=dst, send_sem=send.at[i], recv_sem=recv,
                device_id={"seq": device}, device_id_type=MESH,
            )

        def state_rows(d):
            return pl.ds(pl.multiple_of(d * own_rows, own_rows), own_rows)

        def tot_copy(i):
            return exchange(i, totown, tot.at[s], t_send, t_recv.at[s], peer(i))

        def tot_in(i):
            return exchange(i, totown, tot.at[peer(i)], t_send, t_recv.at[peer(i)], peer(i))

        def first_copy(o, st, rx, send, recv):
            return exchange(o, st.at[state_rows(o), :], rx.at[s], send, recv.at[s], o)

        def first_in(d, st, rx, send, recv):
            return exchange(d, st.at[state_rows(d), :], rx.at[d], send, recv.at[d], d)

        def second_copy(o, out, gi, send, recv):
            return exchange(o, out.at[o], gi.at[state_rows(s), :], send, recv.at[s], o)

        def second_in(d, out, gi, send, recv):
            return exchange(d, out.at[d], gi.at[state_rows(d), :], send, recv.at[d], d)

        def send_head(h, state, st, rx, send, recv):
            st[pl.ds(pl.multiple_of(h * HD, HD), HD), :] = state.astype(BF16)
            for n in range(owners):
                o = h * owners + n

                @pl.when(o != s)
                def _():
                    first_copy(o, st, rx, send, recv).start()

        greeted(3)

        @pl.loop(1, ns)
        def _(i):
            tot_copy(i).start()

        for h in range(nh):
            in_copy(0, h).wait()
            in_copy(1, h).wait()

        def kv_load(h):
            return kb[h], vb[h], cumc[h], [end_of(j, h) for j in range(nb)]

        def kv_work(h, km, vm, cum, ends):
            state = jnp.zeros((HD, HD), F32)
            states = []
            for j in range(nb):
                part = slice(j * blk, (j + 1) * blk)
                states.append(state)
                scaled = (km[part] * jnp.exp(ends[j] - cum[part])).astype(BF16)
                state = jnp.exp(ends[j]) * state + dot_tn(scaled, vm[part])
            return states, state

        def kv_store(h, states, state):
            for j in range(nb):
                floc[j, h] = states[j]
            send_head(h, state, sf, rf, f1_send, f1_recv)

        over_heads(nh, kv_load, kv_work, kv_store, KV_GROUP)

        my_head = (s * own_rows) // HD

        def combine(st, rx, out, gi, order, first, second):
            @pl.loop(1, ns)
            def _(i):
                first_in(peer(i), st, rx, *first).wait_recv()

            rx[s] = st[state_rows(s), :]
            state = jnp.zeros((own_rows, HD), F32)
            for d in order:
                out[d] = state.astype(BF16)
                state = factor[d, 0:1, :] * state + rx[d].astype(F32)

            @pl.loop(1, ns)
            def _(i):
                second_copy(peer(i), out, gi, *second).start()

            gi[state_rows(s), :] = out[s]

        def entry_wait(d, out, gi, second):
            @pl.when(d != s)
            def _():
                second_in(d, out, gi, *second).wait_recv()

        def project(chunks, slots, init=False):
            base = (nb - 1 - chunks[0] // 2) * blk + (chunks[0] % 2) * ch
            rows = pl.ds(base, len(chunks) * ch)

            if init:
                acc[rows, :] = dot_nt(xb[slots[0], rows, :], wb[slots[0]])

            @pl.loop(slots[0] + (1 if init else 0), slots[1])
            def _(r):
                acc[rows, :] += dot_nt(xb[r, rows, :], wb[r])

        def arrived(chunks, slots):
            for k in chunks:
                for r in slots:
                    x_wait(r, k)

        def query_sums(b):
            j = nb - 1 - b
            rows = pl.ds(j * blk, blk)
            for h in range(nh):
                gb[h, rows, :] = acc[rows, h * HD:(h + 1) * HD].astype(BF16)

            def load(h):
                held = None if b == 0 else bcur[h]
                return qb[h, rows, :], gb[h, rows, :], cumc[h, rows, :], end_of(j, h), held

            def work(h, qm, gm, cum, end, held):
                total = dot_tn((qm * jnp.exp(cum)).astype(BF16), gm)
                if b == 0:
                    return jnp.zeros((HD, HD), BF16), total
                return held.astype(BF16), jnp.exp(end) * held + total

            def store(h, entry, total):
                bbf[j, h] = entry
                if b == nb - 1:
                    send_head(h, total, sb, rb, b1_send, b1_recv)
                else:
                    bcur[h] = total

            over_heads(nh, load, work, store)

        def block_terms(b):
            j = nb - 1 - b
            rows = pl.ds(j * blk, blk)

            def load(h):
                mats = [ref[h, rows, :] for ref in (qb, kb, vb, gb)]
                return (*mats, cumc[h, rows, :], cumr[pl.ds(h, 1), rows], end_of(j, h), fbf[j, h], bbf[j, h])

            def work(h, qm, km, vm, gm, cum, cum_row, end, fw, bw):
                gap = cum_row - jnp.concatenate([cum] * (blk // HD), axis=1)
                later = lax.broadcasted_iota(jnp.int32, (blk, blk), 1) >= lax.broadcasted_iota(
                    jnp.int32, (blk, blk), 0
                )
                mask = jnp.where(later, jnp.exp(gap), 0.0)
                gs = (dot_nt(vm, gm) * mask).astype(BF16)
                at = (dot_nt(km, qm) * mask).astype(BF16)
                tail = jnp.exp(end - cum)
                gk = dot_nn(gs, qm) + dot_nt(vm, bw) * tail
                gv = dot_nn(at, gm) + dot_nn(km, bw) * tail
                gq = dot_tn(gs, km) + dot_nt(gm, fw) * jnp.exp(cum)
                return gk, gv, gq.astype(BF16)

            def store(h, gk, gv, gq):
                pk[h, rows, :] = gk
                pv[h, rows, :] = gv
                qb[h, rows, :] = gq

            over_heads(nh, load, work, store)

        fwd = ((f1_send, f1_recv), (f2_send, f2_recv))
        bwd = ((b1_send, b1_recv), (b2_send, b2_recv))

        def near_terms(b):
            pair = (2 * b, 2 * b + 1)
            arrived(pair, (1, 3, 7))
            project(pair, (0, 4), init=True)
            project(pair, (6, 8))

        near(0)

        @pl.loop(1, ns)
        def _(i):
            tot_in(i).wait_recv()

        for d in range(ns):
            factor[d] = jnp.broadcast_to(jnp.exp(tot[d, pl.ds(my_head, 1), :]), (8, HD))
        combine(sf, rf, of, gif, range(ns), *fwd)
        near(1)
        own_copy.wait()
        for h in range(nh):
            in_copy(2, h).wait()
        for r in range(tp):
            w_copy(r).wait()

        for b in range(nb):
            if b > 0:
                near(2 * b)
                near(2 * b + 1)
            if b == 1:
                for d in range(ns):
                    entry_wait(d, of, gif, fwd[1])

                @pl.loop(0, nh)
                def _(h):
                    entry = gif[pl.ds(pl.multiple_of(h * HD, HD), HD), :].astype(F32)
                    prior = jnp.zeros((1, HD), F32)
                    for j in range(nb):
                        fbf[j, h] = (floc[j, h] + jnp.exp(prior) * entry).astype(BF16)
                        prior = prior + end_of(j, h)
            near_terms(b)

        distant(0)
        distant(1)
        for b in range(nb):
            pair = (2 * b, 2 * b + 1)
            if b < nb - 1:
                arrived(pair, (5,))
                project(pair, (4, 6))
                query_sums(b)
                distant(2 * b + 2)
                if b < nb - 2:
                    distant(2 * b + 3)
                if b == 0:
                    block_terms(b)
            else:
                arrived(pair[:1], (5,))
                project(pair[:1], (4, 6))
                distant(pair[1])
                project(pair[1:], (4, 5))
                arrived(pair[1:], (5,))
                project(pair[1:], (5, 6))
                query_sums(b)
        for b in range(1, nb - 1):
            block_terms(b)
        combine(sb, rb, ob, gib, range(ns - 1, -1, -1), *bwd)
        block_terms(nb - 1)
        for d in range(ns):
            entry_wait(d, ob, gib, bwd[1])

        for k in range(nc):
            for n in range(7):
                x_copy(n, k).wait_send()

        @pl.loop(1, ns)
        def _(i):
            tot_copy(i).wait_send()
            d = peer(i)
            first_copy(d, sf, rf, f1_send, f1_recv).wait_send()
            second_copy(d, of, gif, f2_send, f2_recv).wait_send()
            first_copy(d, sb, rb, b1_send, b1_recv).wait_send()
            second_copy(d, ob, gib, b2_send, b2_recv).wait_send()

    dma = pltpu.SemaphoreType.DMA
    scratch = [
        pltpu.VMEM((tp, tok, dp), BF16),
        pltpu.VMEM((tp, nh * HD, dp), BF16),
        pltpu.VMEM((nh, tok, HD), BF16),
        pltpu.VMEM((tok, nh * HD), F32),
        pltpu.VMEM((nh, tok), F32),
        pltpu.VMEM((nh, tok), F32),
        pltpu.VMEM((nb, nh, HD, HD), F32),
        pltpu.VMEM((nb, nh, HD, HD), BF16),
        pltpu.VMEM((nb, nh, HD, HD), BF16),
        pltpu.VMEM((nh, HD, HD), F32),
        pltpu.VMEM((nh * HD, HD), BF16),
        pltpu.VMEM((nh * HD, HD), BF16),
        pltpu.VMEM((ns, own_rows, HD), BF16),
        pltpu.VMEM((ns, own_rows, HD), BF16),
        pltpu.VMEM((ns, own_rows, HD), BF16),
        pltpu.VMEM((ns, own_rows, HD), BF16),
        pltpu.VMEM((nh * HD, HD), BF16),
        pltpu.VMEM((ns, nh, HD), F32),
        pltpu.VMEM((nh, HD), F32),
        pltpu.VMEM((ns, 8, HD), F32),
        dma((7, nc)),
        dma((tp, nc)),
        dma((tp,)),
        dma((3, nh)),
        dma((2,)),
        pltpu.SemaphoreType.REGULAR((4,)),
    ] + [dma((ns,))] * 10
    hbm = pl.BlockSpec(memory_space=pl.ANY)
    vmem = pl.BlockSpec(memory_space=pltpu.VMEM)
    heads = (nh, tok, HD)
    held = [(heads, BF16)] * 3 + [(heads, F32)] * 3 + [((nh * HD, HD), BF16)]
    first = pl.pallas_call(
        kernel,
        out_shape=tuple(pltpu.VMEM(*one) for one in held),
        in_specs=[hbm] * 6,
        out_specs=(vmem,) * len(held),
        scratch_shapes=scratch,
        compiler_params=pltpu.CompilerParams(
            collective_id=0, has_side_effects=True, vmem_limit_bytes=VMEM_FIRST
        ),
    )

    def finish(qb, kb, vb, pk, pv, cumc, gib, gq_hbm, gk_hbm, gv_hbm, kout, vout, out_sem):
        def out_copy(n, h):
            cols = pl.ds(pl.multiple_of(h * HD, HD), HD)
            src, dst = ((qb, gq_hbm), (kout, gk_hbm), (vout, gv_hbm))[n]
            return pltpu.make_async_copy(src.at[h], dst.at[:, cols], out_sem.at[n, h])

        for h in range(nh):
            out_copy(0, h).start()

        def load(h):
            entry = gib[pl.ds(pl.multiple_of(h * HD, HD), HD), :]
            ends = [cumc[h, pl.ds(j * blk + blk - 1, 1), :] for j in range(nb)]
            return kb[h], vb[h], pk[h], pv[h], cumc[h], ends, entry

        def work(h, km, vm, gk, gv, cum, ends, entry):
            after = jnp.zeros((1, HD), F32)
            tails = []
            for j in range(nb - 1, -1, -1):
                after = after + ends[j]
                tails.insert(0, jnp.exp(after - cum[j * blk:(j + 1) * blk]))
            tail = jnp.concatenate(tails, axis=0)
            gk = gk + dot_nt(vm, entry) * tail
            gv = gv + dot_nn(km, entry) * tail
            return gk.astype(BF16), gv.astype(BF16)

        def store(h, gk, gv):
            kout[h] = gk
            vout[h] = gv
            out_copy(1, h).start()
            out_copy(2, h).start()

        over_heads(nh, load, work, store, LAST_GROUP)

        @pl.loop(0, nh)
        def _(h):
            for n in range(3):
                out_copy(n, h).wait()

    out = jax.ShapeDtypeStruct((tok, nh * HD), BF16)
    second = pl.pallas_call(
        finish,
        out_shape=(out, out, out),
        in_specs=[vmem] * len(held),
        out_specs=(hbm, hbm, hbm),
        scratch_shapes=[pltpu.VMEM(heads, BF16), pltpu.VMEM(heads, BF16), dma((3, nh))],
        compiler_params=pltpu.CompilerParams(vmem_limit_bytes=VMEM_SECOND),
    )

    def both(*args):
        kept = first(*args)
        return second(*(pltpu.with_memory_space_constraint(one, pltpu.VMEM) for one in kept))

    return both


def solution(mesh, blk=BLK):
    ns, tp = mesh.shape["seq"], mesh.shape["tp"]

    def local(queries, key_vectors, value_vectors, log_decay, grad_output, out_weight):
        tok, width = queries.shape
        call = make_kernel(ns, tp, tok, width // HD, grad_output.shape[1], blk)
        return call(queries, key_vectors, value_vectors, log_decay, grad_output, out_weight)

    in_specs = (
        P("seq", "tp"),
        P("seq", "tp"),
        P("seq", "tp"),
        P("tp", "seq"),
        P("seq", "tp"),
        P("tp", None),
    )
    out_specs = (P("seq", "tp"), P("seq", "tp"), P("seq", "tp"))
    return jax.shard_map(local, mesh=mesh, in_specs=in_specs, out_specs=out_specs, check_vma=False)
```

```python
import jax
import jax.numpy as jnp
from jax import lax
from jax.experimental import pallas as pl
from jax.experimental.pallas import tpu as pltpu
from jax.sharding import PartitionSpec as P

HD = 128
BLK = 256
MESH = pl.DeviceIdType.MESH
F32 = jnp.float32
BF16 = jnp.bfloat16
VMEM_FIRST = 45000000
VMEM_SECOND = 8000000
LAST_CUTS = 1
GROUP = 4
KV_GROUP = 2
LAST_GROUP = 2


def dot_nn(a, b):
    return lax.dot_general(a, b, (((1,), (0,)), ((), ())), preferred_element_type=F32)


def dot_nt(a, b):
    return lax.dot_general(a, b, (((1,), (1,)), ((), ())), preferred_element_type=F32)


def dot_tn(a, b):
    return lax.dot_general(a, b, (((0,), (0,)), ((), ())), preferred_element_type=F32)


def over_heads(nh, load, work, store, group=GROUP):
    group = min(group, nh)

    @pl.loop(0, nh // group)
    def _(i):
        heads = [i * group + n for n in range(group)]
        done = [work(h, *one) for h, one in zip(heads, [load(h) for h in heads])]
        for h, one in zip(heads, done):
            store(h, *one)


def make_kernel(ns, tp, tok, nh, dp, blk):
    nb = tok // blk
    cuts = [1] * (nb - 1) + [LAST_CUTS]
    chunks = [
        ((nb - 1 - b) * blk + n * (blk // cuts[b]), blk // cuts[b]) for b in range(nb) for n in range(cuts[b])
    ]
    nc = len(chunks)
    last = tuple(range(nb - 1, nc))
    owners = ns // nh
    own_rows = nh * HD // ns

    def kernel(
        q_hbm, k_hbm, v_hbm, ld_hbm, x_hbm, w_hbm,
        qb, kb, vb, pk, pv, cumc, gib,
        xb, wb, gb, acc, ldb, cumr,
        floc, fbf, bbf, bcur, sf, sb, rf, rb, of, ob, gif, tot, totown, factor,
        x_send, x_recv, w_sem, in_sem, ld_sem,
        hello, t_send, t_recv, f1_send, f1_recv, f2_send, f2_recv, b1_send, b1_recv, b2_send, b2_recv,
    ):
        s = lax.axis_index("seq")
        t = lax.axis_index("tp")
        c = lax.rem(t, 2)
        y = t // 2
        up = {"tp": lax.rem(t + 2, tp)}
        down = {"tp": lax.rem(t + tp - 2, tp)}
        sib = {"tp": t + 1 - 2 * c}
        far = {"tp": lax.rem(t + 2 + c * (tp - 4), tp)}
        fslot = 6 - 4 * c
        oslot = 2 + 4 * c

        def peer(i):
            return lax.rem(s + i, ns)

        def head_cols(h):
            return pl.ds(pl.multiple_of(h * HD, HD), HD)

        def in_copy(n, h):
            src = (k_hbm, v_hbm, q_hbm)[n]
            dst = (kb, vb, qb)[n]
            return pltpu.make_async_copy(src.at[:, head_cols(h)], dst.at[h], in_sem.at[n, h])

        def w_copy(r):
            dy, oc = r // 2, r % 2
            piece = lax.rem(y + dy, tp // 2) * 2 + (c if oc == 0 else 1 - c)
            cols = pl.ds(pl.multiple_of(piece * dp, HD), dp)
            return pltpu.make_async_copy(w_hbm.at[:, cols], wb.at[r], w_sem.at[r])

        ld_copy = pltpu.make_async_copy(ld_hbm, ldb, ld_sem.at[0])
        own_copy = pltpu.make_async_copy(x_hbm, xb.at[0], ld_sem.at[1])
        ld_copy.start()
        for n in range(2):
            for h in range(nh):
                in_copy(n, h).start()
        own_copy.start()
        for h in range(nh):
            in_copy(2, h).start()
        for r in range(tp):
            w_copy(r).start()

        inner = 4 if ns % 4 == 0 else ns
        outer = ns // inner
        across, along = s // inner, lax.rem(s, inner)
        beside = []
        for step in (1, inner - 1):
            beside.append({"seq": across * inner + lax.rem(along + step, inner)})
        if outer > 1:
            for step in (1, outer - 1):
                beside.append({"seq": lax.rem(across + step, outer) * inner + along})
        rounds = inner // 2 + outer // 2

        def greet(sem, devices):
            for dev in devices:
                pl.semaphore_signal(sem, inc=1, device_id=dev, device_id_type=MESH)

        barrier = pltpu.get_barrier_semaphore()
        greet(barrier, [up, down, sib] + beside)
        pl.semaphore_wait(barrier, 3 + len(beside))

        def greet_next(r):
            if r < rounds:
                greet(hello.at[r], beside)

        def greeted(r):
            if r < rounds:
                pl.semaphore_wait(hello.at[r], len(beside))

        def rows_of(k):
            return pl.ds(*chunks[k])

        def x_copy(n, k):
            rows = rows_of(k)
            if n < 3:
                src = x_hbm.at[rows, :]
                slot, dev = ((6, up), (2, down), (1, sib))[n]
            else:
                slot, dev, held = (
                    (4, far, fslot), (fslot + 1, sib, fslot), (oslot + 1, sib, oslot), (5, sib, 4)
                )[n - 3]
                src = xb.at[held, rows, :]
            return pltpu.make_async_remote_copy(
                src_ref=src,
                dst_ref=xb.at[slot, rows, :],
                send_sem=x_send.at[n, k],
                recv_sem=x_recv.at[slot, k],
                device_id=dev,
                device_id_type=MESH,
            )

        def x_wait(slot, k):
            rows = rows_of(k)
            pltpu.make_async_remote_copy(
                src_ref=xb.at[slot, rows, :],
                dst_ref=xb.at[slot, rows, :],
                send_sem=x_send.at[0, k],
                recv_sem=x_recv.at[slot, k],
                device_id=sib,
                device_id_type=MESH,
            ).wait_recv()

        def near(k):
            x_wait(fslot, k)
            x_copy(3, k).start()
            x_copy(4, k).start()
            x_wait(oslot, k)
            x_copy(5, k).start()

        def distant(k):
            x_wait(4, k)
            x_copy(6, k).start()

        for k in range(nc):
            for n in range(3):
                x_copy(n, k).start()

        greet_next(1)

        ld_copy.wait()
        greeted(1)
        greet_next(2)
        row_i = lax.broadcasted_iota(jnp.int32, (blk, blk), 0)
        col_i = lax.broadcasted_iota(jnp.int32, (blk, blk), 1)
        tri = jnp.where(col_i <= row_i, 1.0, 0.0).astype(F32)
        for j in range(nb):
            part = ldb[:, j * blk:(j + 1) * blk]
            dims = (((1,), (1,)), ((), ()))
            cumr[:, j * blk:(j + 1) * blk] = lax.dot_general(
                part, tri, dims, precision=lax.Precision.HIGHEST, preferred_element_type=F32
            )
            col = lax.dot_general(
                tri, part, dims, precision=lax.Precision.HIGHEST, preferred_element_type=F32
            )
            for h in range(nh):
                cumc[h, j * blk:(j + 1) * blk, :] = jnp.broadcast_to(col[:, h:h + 1], (blk, HD))

        greeted(2)
        greet_next(3)

        def end_of(j, h):
            return cumc[h, pl.ds(j * blk + blk - 1, 1), :]

        for h in range(nh):
            total = end_of(0, h)
            for j in range(1, nb):
                total = total + end_of(j, h)
            totown[h:h + 1, :] = total
        tot[s] = totown[...]

        def exchange(i, src, dst, send, recv, device):
            return pltpu.make_async_remote_copy(
                src_ref=src, dst_ref=dst, send_sem=send.at[i], recv_sem=recv,
                device_id={"seq": device}, device_id_type=MESH,
            )

        def state_rows(d):
            return pl.ds(pl.multiple_of(d * own_rows, own_rows), own_rows)

        def tot_copy(i):
            return exchange(i, totown, tot.at[s], t_send, t_recv.at[s], peer(i))

        def tot_in(i):
            return exchange(i, totown, tot.at[peer(i)], t_send, t_recv.at[peer(i)], peer(i))

        def first_copy(o, st, rx, send, recv):
            return exchange(o, st.at[state_rows(o), :], rx.at[s], send, recv.at[s], o)

        def first_in(d, st, rx, send, recv):
            return exchange(d, st.at[state_rows(d), :], rx.at[d], send, recv.at[d], d)

        def second_copy(o, out, gi, send, recv):
            return exchange(o, out.at[o], gi.at[state_rows(s), :], send, recv.at[s], o)

        def second_in(d, out, gi, send, recv):
            return exchange(d, out.at[d], gi.at[state_rows(d), :], send, recv.at[d], d)

        def send_head(h, state, st, rx, send, recv):
            st[pl.ds(pl.multiple_of(h * HD, HD), HD), :] = state.astype(BF16)
            for n in range(owners):
                o = h * owners + n

                @pl.when(o != s)
                def _():
                    first_copy(o, st, rx, send, recv).start()

        greeted(3)

        @pl.loop(1, ns)
        def _(i):
            tot_copy(i).start()

        for h in range(nh):
            in_copy(0, h).wait()
            in_copy(1, h).wait()

        def kv_load(h):
            return kb[h], vb[h], cumc[h], [end_of(j, h) for j in range(nb)]

        def kv_work(h, km, vm, cum, ends):
            state = jnp.zeros((HD, HD), F32)
            states = []
            for j in range(nb):
                part = slice(j * blk, (j + 1) * blk)
                states.append(state)
                scaled = (km[part] * jnp.exp(ends[j] - cum[part])).astype(BF16)
                state = jnp.exp(ends[j]) * state + dot_tn(scaled, vm[part])
            return states, state

        def kv_store(h, states, state):
            for j in range(nb):
                floc[j, h] = states[j]
            send_head(h, state, sf, rf, f1_send, f1_recv)

        over_heads(nh, kv_load, kv_work, kv_store, KV_GROUP)

        my_head = (s * own_rows) // HD

        def combine(st, rx, out, gi, order, first, second):
            @pl.loop(1, ns)
            def _(i):
                first_in(peer(i), st, rx, *first).wait_recv()

            rx[s] = st[state_rows(s), :]
            state = jnp.zeros((own_rows, HD), F32)
            for d in order:
                out[d] = state.astype(BF16)
                state = factor[d, 0:1, :] * state + rx[d].astype(F32)

            @pl.loop(1, ns)
            def _(i):
                second_copy(peer(i), out, gi, *second).start()

            gi[state_rows(s), :] = out[s]

        def entry_wait(d, out, gi, second):
            @pl.when(d != s)
            def _():
                second_in(d, out, gi, *second).wait_recv()

        def project(which, slots, init=False):
            rows = pl.ds(chunks[which[0]][0], sum(chunks[k][1] for k in which))

            if init:
                acc[rows, :] = dot_nt(xb[slots[0], rows, :], wb[slots[0]])

            @pl.loop(slots[0] + (1 if init else 0), slots[1])
            def _(r):
                acc[rows, :] += dot_nt(xb[r, rows, :], wb[r])

        def arrived(which, slots):
            for k in which:
                for r in slots:
                    x_wait(r, k)

        def query_sums(b):
            j = nb - 1 - b
            rows = pl.ds(j * blk, blk)
            for h in range(nh):
                gb[h, rows, :] = acc[rows, h * HD:(h + 1) * HD].astype(BF16)

            def load(h):
                held = None if b == 0 else bcur[h]
                return qb[h, rows, :], gb[h, rows, :], cumc[h, rows, :], end_of(j, h), held

            def work(h, qm, gm, cum, end, held):
                total = dot_tn((qm * jnp.exp(cum)).astype(BF16), gm)
                if b == 0:
                    return jnp.zeros((HD, HD), BF16), total
                return held.astype(BF16), jnp.exp(end) * held + total

            def store(h, entry, total):
                bbf[j, h] = entry
                if b == nb - 1:
                    send_head(h, total, sb, rb, b1_send, b1_recv)
                else:
                    bcur[h] = total

            over_heads(nh, load, work, store)

        def block_terms(b):
            j = nb - 1 - b
            rows = pl.ds(j * blk, blk)

            def load(h):
                mats = [ref[h, rows, :] for ref in (qb, kb, vb, gb)]
                return (*mats, cumc[h, rows, :], cumr[pl.ds(h, 1), rows], end_of(j, h), fbf[j, h], bbf[j, h])

            def work(h, qm, km, vm, gm, cum, cum_row, end, fw, bw):
                gap = cum_row - jnp.concatenate([cum] * (blk // HD), axis=1)
                later = lax.broadcasted_iota(jnp.int32, (blk, blk), 1) >= lax.broadcasted_iota(
                    jnp.int32, (blk, blk), 0
                )
                mask = jnp.where(later, jnp.exp(gap), 0.0)
                gs = (dot_nt(vm, gm) * mask).astype(BF16)
                at = (dot_nt(km, qm) * mask).astype(BF16)
                tail = jnp.exp(end - cum)
                gk = dot_nn(gs, qm) + dot_nt(vm, bw) * tail
                gv = dot_nn(at, gm) + dot_nn(km, bw) * tail
                gq = dot_tn(gs, km) + dot_nt(gm, fw) * jnp.exp(cum)
                return gk, gv, gq.astype(BF16)

            def store(h, gk, gv, gq):
                pk[h, rows, :] = gk
                pv[h, rows, :] = gv
                qb[h, rows, :] = gq

            over_heads(nh, load, work, store)

        fwd = ((f1_send, f1_recv), (f2_send, f2_recv))
        bwd = ((b1_send, b1_recv), (b2_send, b2_recv))

        def near_terms(b):
            which = (b,) if b < nb - 1 else last
            arrived(which, (1, 3, 7))
            project(which, (0, 4), init=True)
            project(which, (6, 8))

        near(0)

        @pl.loop(1, ns)
        def _(i):
            tot_in(i).wait_recv()

        for d in range(ns):
            factor[d] = jnp.broadcast_to(jnp.exp(tot[d, pl.ds(my_head, 1), :]), (8, HD))
        combine(sf, rf, of, gif, range(ns), *fwd)
        own_copy.wait()
        for h in range(nh):
            in_copy(2, h).wait()
        for r in range(tp):
            w_copy(r).wait()

        for b in range(nb):
            if b > 0:
                for k in (b,) if b < nb - 1 else last:
                    near(k)
            if b == 1:
                for d in range(ns):
                    entry_wait(d, of, gif, fwd[1])

                @pl.loop(0, nh)
                def _(h):
                    entry = gif[pl.ds(pl.multiple_of(h * HD, HD), HD), :].astype(F32)
                    prior = jnp.zeros((1, HD), F32)
                    for j in range(nb):
                        fbf[j, h] = (floc[j, h] + jnp.exp(prior) * entry).astype(BF16)
                        prior = prior + end_of(j, h)
            near_terms(b)

        distant(0)
        for b in range(nb - 1):
            arrived((b,), (5,))
            project((b,), (4, 6))
            query_sums(b)
            distant(b + 1)
            if b == 0:
                block_terms(b)
        for k in last:
            if k > last[0]:
                distant(k)
                project((k,), (4, 5))
                arrived((k,), (5,))
                project((k,), (5, 6))
            elif k == last[-1]:
                project((k,), (4, 5))
                arrived((k,), (5,))
                project((k,), (5, 6))
            else:
                arrived((k,), (5,))
                project((k,), (4, 6))
        query_sums(nb - 1)
        for b in range(1, nb - 1):
            block_terms(b)
        combine(sb, rb, ob, gib, range(ns - 1, -1, -1), *bwd)
        block_terms(nb - 1)
        for d in range(ns):
            entry_wait(d, ob, gib, bwd[1])

        for k in range(nc):
            for n in range(7):
                x_copy(n, k).wait_send()

        @pl.loop(1, ns)
        def _(i):
            tot_copy(i).wait_send()
            d = peer(i)
            first_copy(d, sf, rf, f1_send, f1_recv).wait_send()
            second_copy(d, of, gif, f2_send, f2_recv).wait_send()
            first_copy(d, sb, rb, b1_send, b1_recv).wait_send()
            second_copy(d, ob, gib, b2_send, b2_recv).wait_send()

    dma = pltpu.SemaphoreType.DMA
    scratch = [
        pltpu.VMEM((tp, tok, dp), BF16),
        pltpu.VMEM((tp, nh * HD, dp), BF16),
        pltpu.VMEM((nh, tok, HD), BF16),
        pltpu.VMEM((tok, nh * HD), F32),
        pltpu.VMEM((nh, tok), F32),
        pltpu.VMEM((nh, tok), F32),
        pltpu.VMEM((nb, nh, HD, HD), F32),
        pltpu.VMEM((nb, nh, HD, HD), BF16),
        pltpu.VMEM((nb, nh, HD, HD), BF16),
        pltpu.VMEM((nh, HD, HD), F32),
        pltpu.VMEM((nh * HD, HD), BF16),
        pltpu.VMEM((nh * HD, HD), BF16),
        pltpu.VMEM((ns, own_rows, HD), BF16),
        pltpu.VMEM((ns, own_rows, HD), BF16),
        pltpu.VMEM((ns, own_rows, HD), BF16),
        pltpu.VMEM((ns, own_rows, HD), BF16),
        pltpu.VMEM((nh * HD, HD), BF16),
        pltpu.VMEM((ns, nh, HD), F32),
        pltpu.VMEM((nh, HD), F32),
        pltpu.VMEM((ns, 8, HD), F32),
        dma((7, nc)),
        dma((tp, nc)),
        dma((tp,)),
        dma((3, nh)),
        dma((2,)),
        pltpu.SemaphoreType.REGULAR((4,)),
    ] + [dma((ns,))] * 10
    hbm = pl.BlockSpec(memory_space=pl.ANY)
    vmem = pl.BlockSpec(memory_space=pltpu.VMEM)
    heads = (nh, tok, HD)
    held = [(heads, BF16)] * 3 + [(heads, F32)] * 3 + [((nh * HD, HD), BF16)]
    first = pl.pallas_call(
        kernel,
        out_shape=tuple(pltpu.VMEM(*one) for one in held),
        in_specs=[hbm] * 6,
        out_specs=(vmem,) * len(held),
        scratch_shapes=scratch,
        compiler_params=pltpu.CompilerParams(
            collective_id=0, has_side_effects=True, vmem_limit_bytes=VMEM_FIRST
        ),
    )

    def finish(qb, kb, vb, pk, pv, cumc, gib, gq_hbm, gk_hbm, gv_hbm, kout, vout, out_sem):
        def out_copy(n, h):
            cols = pl.ds(pl.multiple_of(h * HD, HD), HD)
            src, dst = ((qb, gq_hbm), (kout, gk_hbm), (vout, gv_hbm))[n]
            return pltpu.make_async_copy(src.at[h], dst.at[:, cols], out_sem.at[n, h])

        for h in range(nh):
            out_copy(0, h).start()

        def load(h):
            entry = gib[pl.ds(pl.multiple_of(h * HD, HD), HD), :]
            ends = [cumc[h, pl.ds(j * blk + blk - 1, 1), :] for j in range(nb)]
            return kb[h], vb[h], pk[h], pv[h], cumc[h], ends, entry

        def work(h, km, vm, gk, gv, cum, ends, entry):
            after = jnp.zeros((1, HD), F32)
            tails = []
            for j in range(nb - 1, -1, -1):
                after = after + ends[j]
                tails.insert(0, jnp.exp(after - cum[j * blk:(j + 1) * blk]))
            tail = jnp.concatenate(tails, axis=0)
            gk = gk + dot_nt(vm, entry) * tail
            gv = gv + dot_nn(km, entry) * tail
            return gk.astype(BF16), gv.astype(BF16)

        def store(h, gk, gv):
            kout[h] = gk
            vout[h] = gv
            out_copy(1, h).start()
            out_copy(2, h).start()

        over_heads(nh, load, work, store, LAST_GROUP)

        @pl.loop(0, nh)
        def _(h):
            for n in range(3):
                out_copy(n, h).wait()

    out = jax.ShapeDtypeStruct((tok, nh * HD), BF16)
    second = pl.pallas_call(
        finish,
        out_shape=(out, out, out),
        in_specs=[vmem] * len(held),
        out_specs=(hbm, hbm, hbm),
        scratch_shapes=[pltpu.VMEM(heads, BF16), pltpu.VMEM(heads, BF16), dma((3, nh))],
        compiler_params=pltpu.CompilerParams(vmem_limit_bytes=VMEM_SECOND),
    )

    def both(*args):
        kept = first(*args)
        return second(*(pltpu.with_memory_space_constraint(one, pltpu.VMEM) for one in kept))

    return both


def solution(mesh, blk=BLK):
    ns, tp = mesh.shape["seq"], mesh.shape["tp"]

    def local(queries, key_vectors, value_vectors, log_decay, grad_output, out_weight):
        tok, width = queries.shape
        call = make_kernel(ns, tp, tok, width // HD, grad_output.shape[1], blk)
        return call(queries, key_vectors, value_vectors, log_decay, grad_output, out_weight)

    in_specs = (
        P("seq", "tp"),
        P("seq", "tp"),
        P("seq", "tp"),
        P("tp", "seq"),
        P("seq", "tp"),
        P("tp", None),
    )
    out_specs = (P("seq", "tp"), P("seq", "tp"), P("seq", "tp"))
    return jax.shard_map(local, mesh=mesh, in_specs=in_specs, out_specs=out_specs, check_vma=False)
```

```python
import jax
import jax.numpy as jnp
from jax import lax
from jax.experimental import pallas as pl
from jax.experimental.pallas import tpu as pltpu
from jax.sharding import PartitionSpec as P

HD = 128
BLK = 256
MESH = pl.DeviceIdType.MESH
F32 = jnp.float32
BF16 = jnp.bfloat16
VMEM_FIRST = 45000000
VMEM_SECOND = 8000000
LAST_CUTS = 1
GROUP = 4
KV_GROUP = 2
LAST_GROUP = 2


def dot_nn(a, b):
    return lax.dot_general(a, b, (((1,), (0,)), ((), ())), preferred_element_type=F32)


def dot_nt(a, b):
    return lax.dot_general(a, b, (((1,), (1,)), ((), ())), preferred_element_type=F32)


def dot_tn(a, b):
    return lax.dot_general(a, b, (((0,), (0,)), ((), ())), preferred_element_type=F32)


def over_heads(nh, load, work, store, group=GROUP):
    group = min(group, nh)

    @pl.loop(0, nh // group)
    def _(i):
        heads = [i * group + n for n in range(group)]
        done = [work(h, *one) for h, one in zip(heads, [load(h) for h in heads])]
        for h, one in zip(heads, done):
            store(h, *one)


def make_kernel(ns, tp, tok, nh, dp, blk):
    nb = tok // blk
    cuts = [1] * (nb - 1) + [LAST_CUTS]
    chunks = [
        ((nb - 1 - b) * blk + n * (blk // cuts[b]), blk // cuts[b]) for b in range(nb) for n in range(cuts[b])
    ]
    nc = len(chunks)
    last = tuple(range(nb - 1, nc))
    owners = ns // nh
    own_rows = nh * HD // ns

    def kernel(
        q_hbm, k_hbm, v_hbm, ld_hbm, x_hbm, w_hbm,
        qb, kb, vb, pk, pv, cumc, gib,
        xb, wb, gb, acc, ldb, cumr,
        floc, fbf, bbf, bcur, sf, sb, rf, rb, of, ob, gif, tot, totown, factor,
        x_send, x_recv, w_sem, in_sem, ld_sem,
        hello, t_send, t_recv, f1_send, f1_recv, f2_send, f2_recv, b1_send, b1_recv, b2_send, b2_recv,
    ):
        s = lax.axis_index("seq")
        t = lax.axis_index("tp")
        c = lax.rem(t, 2)
        y = t // 2
        up = {"tp": lax.rem(t + 2, tp)}
        down = {"tp": lax.rem(t + tp - 2, tp)}
        sib = {"tp": t + 1 - 2 * c}
        far = {"tp": lax.rem(t + 2 + c * (tp - 4), tp)}
        fslot = 6 - 4 * c
        oslot = 2 + 4 * c

        def peer(i):
            return lax.rem(s + i, ns)

        def head_cols(h):
            return pl.ds(pl.multiple_of(h * HD, HD), HD)

        def in_copy(n, h):
            src = (k_hbm, v_hbm, q_hbm)[n]
            dst = (kb, vb, qb)[n]
            return pltpu.make_async_copy(src.at[:, head_cols(h)], dst.at[h], in_sem.at[n, h])

        def w_copy(r):
            dy, oc = r // 2, r % 2
            piece = lax.rem(y + dy, tp // 2) * 2 + (c if oc == 0 else 1 - c)
            cols = pl.ds(pl.multiple_of(piece * dp, HD), dp)
            return pltpu.make_async_copy(w_hbm.at[:, cols], wb.at[r], w_sem.at[r])

        ld_copy = pltpu.make_async_copy(ld_hbm, ldb, ld_sem.at[0])
        own_copy = pltpu.make_async_copy(x_hbm, xb.at[0], ld_sem.at[1])
        ld_copy.start()
        for n in range(2):
            for h in range(nh):
                in_copy(n, h).start()
        own_copy.start()
        for h in range(nh):
            in_copy(2, h).start()
        for r in range(tp):
            w_copy(r).start()

        inner = 4 if ns % 4 == 0 else ns
        outer = ns // inner
        across, along = s // inner, lax.rem(s, inner)
        beside = []
        for step in (1, inner - 1):
            beside.append({"seq": across * inner + lax.rem(along + step, inner)})
        if outer > 1:
            for step in (1, outer - 1):
                beside.append({"seq": lax.rem(across + step, outer) * inner + along})
        rounds = inner // 2 + outer // 2

        def greet(sem, devices):
            for dev in devices:
                pl.semaphore_signal(sem, inc=1, device_id=dev, device_id_type=MESH)

        barrier = pltpu.get_barrier_semaphore()
        greet(barrier, [up, down, sib] + beside)
        pl.semaphore_wait(barrier, 3 + len(beside))

        def greet_next(r):
            if r < rounds:
                greet(hello.at[r], beside)

        def greeted(r):
            if r < rounds:
                pl.semaphore_wait(hello.at[r], len(beside))

        def rows_of(k):
            return pl.ds(*chunks[k])

        def x_copy(n, k):
            rows = rows_of(k)
            if n < 3:
                src = x_hbm.at[rows, :]
                slot, dev = ((6, up), (2, down), (1, sib))[n]
            else:
                slot, dev, held = (
                    (4, far, fslot), (fslot + 1, sib, fslot), (oslot + 1, sib, oslot), (5, sib, 4)
                )[n - 3]
                src = xb.at[held, rows, :]
            return pltpu.make_async_remote_copy(
                src_ref=src,
                dst_ref=xb.at[slot, rows, :],
                send_sem=x_send.at[n, k],
                recv_sem=x_recv.at[slot, k],
                device_id=dev,
                device_id_type=MESH,
            )

        def x_wait(slot, k):
            rows = rows_of(k)
            pltpu.make_async_remote_copy(
                src_ref=xb.at[slot, rows, :],
                dst_ref=xb.at[slot, rows, :],
                send_sem=x_send.at[0, k],
                recv_sem=x_recv.at[slot, k],
                device_id=sib,
                device_id_type=MESH,
            ).wait_recv()

        def near(k):
            x_wait(fslot, k)
            x_copy(3, k).start()
            x_copy(4, k).start()
            x_wait(oslot, k)
            x_copy(5, k).start()

        def distant(k):
            x_wait(4, k)
            x_copy(6, k).start()

        for k in range(nc):
            for n in range(3):
                x_copy(n, k).start()

        greet_next(1)

        ld_copy.wait()
        greeted(1)
        greet_next(2)
        row_i = lax.broadcasted_iota(jnp.int32, (blk, blk), 0)
        col_i = lax.broadcasted_iota(jnp.int32, (blk, blk), 1)
        tri = jnp.where(col_i <= row_i, 1.0, 0.0).astype(F32)
        for j in range(nb):
            part = ldb[:, j * blk:(j + 1) * blk]
            dims = (((1,), (1,)), ((), ()))
            cumr[:, j * blk:(j + 1) * blk] = lax.dot_general(
                part, tri, dims, precision=lax.Precision.HIGHEST, preferred_element_type=F32
            )
            col = lax.dot_general(
                tri, part, dims, precision=lax.Precision.HIGHEST, preferred_element_type=F32
            )
            for h in range(nh):
                cumc[h, j * blk:(j + 1) * blk, :] = jnp.broadcast_to(col[:, h:h + 1], (blk, HD))

        greeted(2)
        greet_next(3)

        def end_of(j, h):
            return cumc[h, pl.ds(j * blk + blk - 1, 1), :]

        for h in range(nh):
            total = end_of(0, h)
            for j in range(1, nb):
                total = total + end_of(j, h)
            totown[h:h + 1, :] = total
        tot[s] = totown[...]

        def exchange(i, src, dst, send, recv, device):
            return pltpu.make_async_remote_copy(
                src_ref=src, dst_ref=dst, send_sem=send.at[i], recv_sem=recv,
                device_id={"seq": device}, device_id_type=MESH,
            )

        def state_rows(d):
            return pl.ds(pl.multiple_of(d * own_rows, own_rows), own_rows)

        def tot_copy(i):
            return exchange(i, totown, tot.at[s], t_send, t_recv.at[s], peer(i))

        def tot_in(i):
            return exchange(i, totown, tot.at[peer(i)], t_send, t_recv.at[peer(i)], peer(i))

        def first_copy(o, st, rx, send, recv):
            return exchange(o, st.at[state_rows(o), :], rx.at[s], send, recv.at[s], o)

        def first_in(d, st, rx, send, recv):
            return exchange(d, st.at[state_rows(d), :], rx.at[d], send, recv.at[d], d)

        def second_copy(o, out, gi, send, recv):
            return exchange(o, out.at[o], gi.at[state_rows(s), :], send, recv.at[s], o)

        def second_in(d, out, gi, send, recv):
            return exchange(d, out.at[d], gi.at[state_rows(d), :], send, recv.at[d], d)

        def send_head(h, state, st, rx, send, recv):
            st[pl.ds(pl.multiple_of(h * HD, HD), HD), :] = state.astype(BF16)
            for n in range(owners):
                o = h * owners + n

                @pl.when(o != s)
                def _():
                    first_copy(o, st, rx, send, recv).start()

        greeted(3)

        @pl.loop(1, ns)
        def _(i):
            tot_copy(i).start()

        for h in range(nh):
            in_copy(0, h).wait()
            in_copy(1, h).wait()

        def kv_load(h):
            return kb[h], vb[h], cumc[h], [end_of(j, h) for j in range(nb)]

        def kv_work(h, km, vm, cum, ends):
            state = jnp.zeros((HD, HD), F32)
            states = []
            for j in range(nb):
                part = slice(j * blk, (j + 1) * blk)
                states.append(state)
                scaled = (km[part] * jnp.exp(ends[j] - cum[part])).astype(BF16)
                state = jnp.exp(ends[j]) * state + dot_tn(scaled, vm[part])
            return states, state

        def kv_store(h, states, state):
            for j in range(nb):
                floc[j, h] = states[j]
            send_head(h, state, sf, rf, f1_send, f1_recv)

        over_heads(nh, kv_load, kv_work, kv_store, KV_GROUP)

        my_head = (s * own_rows) // HD

        def combine(st, rx, out, gi, order, first, second):
            @pl.loop(1, ns)
            def _(i):
                first_in(peer(i), st, rx, *first).wait_recv()

            rx[s] = st[state_rows(s), :]
            state = jnp.zeros((own_rows, HD), F32)
            for d in order:
                out[d] = state.astype(BF16)
                state = factor[d, 0:1, :] * state + rx[d].astype(F32)

            @pl.loop(1, ns)
            def _(i):
                second_copy(peer(i), out, gi, *second).start()

            gi[state_rows(s), :] = out[s]

        def entry_wait(d, out, gi, second):
            @pl.when(d != s)
            def _():
                second_in(d, out, gi, *second).wait_recv()

        def project(which, slots, init=False):
            rows = pl.ds(chunks[which[0]][0], sum(chunks[k][1] for k in which))

            if init:
                acc[rows, :] = dot_nt(xb[slots[0], rows, :], wb[slots[0]])

            @pl.loop(slots[0] + (1 if init else 0), slots[1])
            def _(r):
                acc[rows, :] += dot_nt(xb[r, rows, :], wb[r])

        def arrived(which, slots):
            for k in which:
                for r in slots:
                    x_wait(r, k)

        def query_sums(b):
            j = nb - 1 - b
            rows = pl.ds(j * blk, blk)
            for h in range(nh):
                gb[h, rows, :] = acc[rows, h * HD:(h + 1) * HD].astype(BF16)

            def load(h):
                held = None if b == 0 else bcur[h]
                return qb[h, rows, :], gb[h, rows, :], cumc[h, rows, :], end_of(j, h), held

            def work(h, qm, gm, cum, end, held):
                total = dot_tn((qm * jnp.exp(cum)).astype(BF16), gm)
                if b == 0:
                    return jnp.zeros((HD, HD), BF16), total
                return held.astype(BF16), jnp.exp(end) * held + total

            def store(h, entry, total):
                bbf[j, h] = entry
                if b == nb - 1:
                    send_head(h, total, sb, rb, b1_send, b1_recv)
                else:
                    bcur[h] = total

            over_heads(nh, load, work, store)

        def block_terms(b):
            j = nb - 1 - b
            rows = pl.ds(j * blk, blk)

            def load(h):
                mats = [ref[h, rows, :] for ref in (qb, kb, vb, gb)]
                return (*mats, cumc[h, rows, :], cumr[pl.ds(h, 1), rows], end_of(j, h), fbf[j, h], bbf[j, h])

            def work(h, qm, km, vm, gm, cum, cum_row, end, fw, bw):
                gap = cum_row - jnp.concatenate([cum] * (blk // HD), axis=1)
                later = lax.broadcasted_iota(jnp.int32, (blk, blk), 1) >= lax.broadcasted_iota(
                    jnp.int32, (blk, blk), 0
                )
                mask = jnp.where(later, jnp.exp(gap), 0.0)
                gs = (dot_nt(vm, gm) * mask).astype(BF16)
                at = (dot_nt(km, qm) * mask).astype(BF16)
                tail = jnp.exp(end - cum)
                gk = dot_nn(gs, qm) + dot_nt(vm, bw) * tail
                gv = dot_nn(at, gm) + dot_nn(km, bw) * tail
                gq = dot_tn(gs, km) + dot_nt(gm, fw) * jnp.exp(cum)
                return gk, gv, gq.astype(BF16)

            def store(h, gk, gv, gq):
                pk[h, rows, :] = gk
                pv[h, rows, :] = gv
                qb[h, rows, :] = gq

            over_heads(nh, load, work, store)

        fwd = ((f1_send, f1_recv), (f2_send, f2_recv))
        bwd = ((b1_send, b1_recv), (b2_send, b2_recv))

        def near_terms(b):
            which = (b,) if b < nb - 1 else last
            arrived(which, (1, 3, 7))
            project(which, (0, 4), init=True)
            project(which, (6, 8))

        near(0)

        @pl.loop(1, ns)
        def _(i):
            tot_in(i).wait_recv()

        for d in range(ns):
            factor[d] = jnp.broadcast_to(jnp.exp(tot[d, pl.ds(my_head, 1), :]), (8, HD))
        combine(sf, rf, of, gif, range(ns), *fwd)
        own_copy.wait()
        for h in range(nh):
            in_copy(2, h).wait()
        for r in range(tp):
            w_copy(r).wait()

        for b in range(nb):
            if b > 0:
                for k in (b,) if b < nb - 1 else last:
                    near(k)
            if b == 1:
                for d in range(ns):
                    entry_wait(d, of, gif, fwd[1])

                @pl.loop(0, nh)
                def _(h):
                    entry = gif[pl.ds(pl.multiple_of(h * HD, HD), HD), :].astype(F32)
                    prior = jnp.zeros((1, HD), F32)
                    for j in range(nb):
                        fbf[j, h] = (floc[j, h] + jnp.exp(prior) * entry).astype(BF16)
                        prior = prior + end_of(j, h)
            near_terms(b)

        distant(0)
        for b in range(nb - 1):
            arrived((b,), (5,))
            project((b,), (4, 6))
            query_sums(b)
            distant(b + 1)
            if b == 0:
                block_terms(b)
        for k in last:
            if k > last[0]:
                distant(k)
                project((k,), (4, 5))
                arrived((k,), (5,))
                project((k,), (5, 6))
            elif k == last[-1]:
                project((k,), (4, 5))
                arrived((k,), (5,))
                project((k,), (5, 6))
            else:
                arrived((k,), (5,))
                project((k,), (4, 6))
        query_sums(nb - 1)
        for b in range(1, nb - 1):
            block_terms(b)
        combine(sb, rb, ob, gib, range(ns - 1, -1, -1), *bwd)
        block_terms(nb - 1)

        for k in range(nc):
            for n in range(7):
                x_copy(n, k).wait_send()

        @pl.loop(1, ns)
        def _(i):
            tot_copy(i).wait_send()
            d = peer(i)
            first_copy(d, sf, rf, f1_send, f1_recv).wait_send()
            second_copy(d, of, gif, f2_send, f2_recv).wait_send()
            first_copy(d, sb, rb, b1_send, b1_recv).wait_send()

        @pl.loop(1, ns)
        def _(i):
            second_in(peer(i), ob, gib, b2_send, b2_recv).wait_recv()

        @pl.loop(1, ns)
        def _(i):
            second_copy(peer(i), ob, gib, b2_send, b2_recv).wait_send()

    dma = pltpu.SemaphoreType.DMA
    scratch = [
        pltpu.VMEM((tp, tok, dp), BF16),
        pltpu.VMEM((tp, nh * HD, dp), BF16),
        pltpu.VMEM((nh, tok, HD), BF16),
        pltpu.VMEM((tok, nh * HD), F32),
        pltpu.VMEM((nh, tok), F32),
        pltpu.VMEM((nh, tok), F32),
        pltpu.VMEM((nb, nh, HD, HD), F32),
        pltpu.VMEM((nb, nh, HD, HD), BF16),
        pltpu.VMEM((nb, nh, HD, HD), BF16),
        pltpu.VMEM((nh, HD, HD), F32),
        pltpu.VMEM((nh * HD, HD), BF16),
        pltpu.VMEM((nh * HD, HD), BF16),
        pltpu.VMEM((ns, own_rows, HD), BF16),
        pltpu.VMEM((ns, own_rows, HD), BF16),
        pltpu.VMEM((ns, own_rows, HD), BF16),
        pltpu.VMEM((ns, own_rows, HD), BF16),
        pltpu.VMEM((nh * HD, HD), BF16),
        pltpu.VMEM((ns, nh, HD), F32),
        pltpu.VMEM((nh, HD), F32),
        pltpu.VMEM((ns, 8, HD), F32),
        dma((7, nc)),
        dma((tp, nc)),
        dma((tp,)),
        dma((3, nh)),
        dma((2,)),
        pltpu.SemaphoreType.REGULAR((4,)),
    ] + [dma((ns,))] * 10
    hbm = pl.BlockSpec(memory_space=pl.ANY)
    vmem = pl.BlockSpec(memory_space=pltpu.VMEM)
    heads = (nh, tok, HD)
    held = [(heads, BF16)] * 3 + [(heads, F32)] * 3 + [((nh * HD, HD), BF16)]
    first = pl.pallas_call(
        kernel,
        out_shape=tuple(pltpu.VMEM(*one) for one in held),
        in_specs=[hbm] * 6,
        out_specs=(vmem,) * len(held),
        scratch_shapes=scratch,
        compiler_params=pltpu.CompilerParams(
            collective_id=0, has_side_effects=True, vmem_limit_bytes=VMEM_FIRST
        ),
    )

    def finish(qb, kb, vb, pk, pv, cumc, gib, gq_hbm, gk_hbm, gv_hbm, kout, vout, out_sem):
        def out_copy(n, h):
            cols = pl.ds(pl.multiple_of(h * HD, HD), HD)
            src, dst = ((qb, gq_hbm), (kout, gk_hbm), (vout, gv_hbm))[n]
            return pltpu.make_async_copy(src.at[h], dst.at[:, cols], out_sem.at[n, h])

        for h in range(nh):
            out_copy(0, h).start()

        def load(h):
            entry = gib[pl.ds(pl.multiple_of(h * HD, HD), HD), :]
            ends = [cumc[h, pl.ds(j * blk + blk - 1, 1), :] for j in range(nb)]
            return kb[h], vb[h], pk[h], pv[h], cumc[h], ends, entry

        def work(h, km, vm, gk, gv, cum, ends, entry):
            after = jnp.zeros((1, HD), F32)
            tails = []
            for j in range(nb - 1, -1, -1):
                after = after + ends[j]
                tails.insert(0, jnp.exp(after - cum[j * blk:(j + 1) * blk]))
            tail = jnp.concatenate(tails, axis=0)
            gk = gk + dot_nt(vm, entry) * tail
            gv = gv + dot_nn(km, entry) * tail
            return gk.astype(BF16), gv.astype(BF16)

        def store(h, gk, gv):
            kout[h] = gk
            vout[h] = gv
            out_copy(1, h).start()
            out_copy(2, h).start()

        over_heads(nh, load, work, store, LAST_GROUP)

        @pl.loop(0, nh)
        def _(h):
            for n in range(3):
                out_copy(n, h).wait()

    out = jax.ShapeDtypeStruct((tok, nh * HD), BF16)
    second = pl.pallas_call(
        finish,
        out_shape=(out, out, out),
        in_specs=[vmem] * len(held),
        out_specs=(hbm, hbm, hbm),
        scratch_shapes=[pltpu.VMEM(heads, BF16), pltpu.VMEM(heads, BF16), dma((3, nh))],
        compiler_params=pltpu.CompilerParams(vmem_limit_bytes=VMEM_SECOND),
    )

    def both(*args):
        kept = first(*args)
        return second(*(pltpu.with_memory_space_constraint(one, pltpu.VMEM) for one in kept))

    return both


def solution(mesh, blk=BLK):
    ns, tp = mesh.shape["seq"], mesh.shape["tp"]

    def local(queries, key_vectors, value_vectors, log_decay, grad_output, out_weight):
        tok, width = queries.shape
        call = make_kernel(ns, tp, tok, width // HD, grad_output.shape[1], blk)
        return call(queries, key_vectors, value_vectors, log_decay, grad_output, out_weight)

    in_specs = (
        P("seq", "tp"),
        P("seq", "tp"),
        P("seq", "tp"),
        P("tp", "seq"),
        P("seq", "tp"),
        P("tp", None),
    )
    out_specs = (P("seq", "tp"), P("seq", "tp"), P("seq", "tp"))
    return jax.shard_map(local, mesh=mesh, in_specs=in_specs, out_specs=out_specs, check_vma=False)
```
